32 devices in a mesh: scene: 2 (over y), lines: 16 (over z, x, core).
Axes of the slice: x: 2, y: 2, z: 4, core: 2. Of those that a mesh axis runs over, the one named last changes fastest.
Arguments:
- pixels: bfloat16 [1024, 128, 256], P(('scene', 'lines')), parts along dimension 0, may hold values from -100 to 100
- scene_lines: int32 [2], P('scene'), parts along dimension 0, may hold values from 385 to 512
- scene_cols: int32 [2], P('scene'), parts along dimension 0, may hold values from 33 to 128
Outputs:
- anomaly: float32 [1024, 128], P(('scene', 'lines')), parts along dimension 0
The draws below stay inside these ranges and needn't reach their ends.
There are 2 independent parts, one for each index of `scene`. The reference program is written for one: setup_inputs(seed, part) draws one part's arguments, and reference() takes and returns one part's arrays. A program takes and returns all parts, laid end to end along the dimension named above; each array names one. Nothing has to cross between parts.
Inputs may be any that keep to these rules, and one draw needn't show every extreme that they name: The scene occupies the first scene_lines lines of the array. The scene occupies the first scene_cols columns of every line.
All inputs are finite; a program needn't handle non-finite values.
Results may differ from the reference program's by a relative error of at most 0.0003.
Values may be sent and summed in bfloat16 or wider, within the bound.
No kernel may reach another device: no remote copies, remote signals or barrier semaphores. Data moves between devices by JAX's collectives and lax.ppermute only.
A program may use at most 64 MiB of HBM per device.

```python
import math
import jax
import jax.numpy as jnp
from jax import lax

BANDS = 256
COLS = 128
LINES_DEV = 32
OUTER = 32
GUARD = 4
LINES = 512


def smooth_background(key):
    keys = jax.random.split(jax.random.fold_in(key, 29), 4)
    line_period = jnp.exp(jax.random.uniform(keys[0], (4,), jnp.float32, math.log(8.0 * OUTER), math.log(32.0 * OUTER)))
    col_period = jnp.exp(jax.random.uniform(keys[1], (4,), jnp.float32, math.log(2.0 * COLS), math.log(4.0 * COLS)))
    phases = jax.random.uniform(keys[2], (2, 4), jnp.float32, 0.0, 2.0 * math.pi)
    weights = 0.375 * jax.random.uniform(keys[3], (4, BANDS), jnp.float32, -1.0, 1.0)
    line_pos = jnp.arange(LINES, dtype=jnp.float32)
    col_pos = jnp.arange(COLS, dtype=jnp.float32)
    line_wave = jnp.cos(2.0 * math.pi * line_pos[:, None] / line_period[None, :] + phases[0][None, :])
    col_wave = jnp.cos(2.0 * math.pi * col_pos[:, None] / col_period[None, :] + phases[1][None, :])
    return jnp.einsum('lk,ck,kb->lcb', line_wave, col_wave, weights, precision=lax.Precision.HIGHEST)


def draw_pixels(key, part):
    keys = jax.random.split(jax.random.fold_in(key, 11), 7)
    band_scale = jnp.exp(jax.random.uniform(keys[0], (BANDS,), jnp.float32, jnp.log(0.3), jnp.log(3.0)))
    position = jnp.arange(LINES, dtype=jnp.float32) / max(LINES - 1, 1)
    ramp = 1.0 + 2.0 * position
    background = smooth_background(keys[4]) * ramp[:, None, None] * band_scale
    level_sign = jnp.where(jax.random.uniform(keys[5], (BANDS,), jnp.float32) < 0.5, -1.0, 1.0)
    level = level_sign * jax.random.uniform(keys[6], (BANDS,), jnp.float32, 0.5, 1.5) * band_scale
    base = jax.random.truncated_normal(keys[1], -4.0, 4.0, (LINES, COLS, BANDS), jnp.float32)
    values = base * ramp[:, None, None] * band_scale + background + 1.5 * ramp[:, None, None] * level
    return values.astype(jnp.bfloat16)


def setup_inputs(seed: int = 0, part: int = 0) -> dict:
    key_list = jax.random.split(jax.random.key(seed), 4)
    part_splits = jax.random.split(jax.random.fold_in(key_list[3], part), 4)
    pixels = draw_pixels(jax.random.fold_in(jax.random.fold_in(key_list[3], part), 71), part)
    scene_lines = jax.random.randint(part_splits[1], (1,), LINES - 4 * LINES_DEV + 1, LINES + 1).astype(jnp.int32)
    scene_cols = jax.random.randint(part_splits[2], (1,), COLS // 4 + 1, COLS + 1).astype(jnp.int32)
    return {"pixels": pixels, "scene_lines": scene_lines, "scene_cols": scene_cols}


def window_matrix(rows_out, rows_in, offset, radius):
    row_index = lax.broadcasted_iota(jnp.int32, (rows_out, rows_in), 0)
    col_index = lax.broadcasted_iota(jnp.int32, (rows_out, rows_in), 1)
    return jnp.abs(col_index - offset - row_index) <= radius

def cycle_part(source, offset, lines_here):
    lines_in, cols_here, band_count = source.shape
    flat_source = source.reshape(lines_in, cols_here * band_count)
    outer_lines = window_matrix(lines_here, lines_in, offset, OUTER).astype(jnp.bfloat16)
    guard_lines = window_matrix(lines_here, lines_in, offset, GUARD).astype(jnp.bfloat16)
    outer_sum = jnp.dot(outer_lines.astype(jnp.float32), flat_source.astype(jnp.float32), preferred_element_type=jnp.float32).reshape(lines_here, cols_here, band_count)
    guard_sum = jnp.dot(guard_lines.astype(jnp.float32), flat_source.astype(jnp.float32), preferred_element_type=jnp.float32).reshape(lines_here, cols_here, band_count)
    outer_cols = window_matrix(cols_here, cols_here, 0, OUTER).astype(jnp.float32)
    guard_cols = window_matrix(cols_here, cols_here, 0, GUARD).astype(jnp.float32)
    first = jnp.einsum('cd,ldb->lcb', outer_cols, outer_sum, precision=lax.Precision.HIGHEST)
    second = jnp.einsum('cd,ldb->lcb', guard_cols, guard_sum, precision=lax.Precision.HIGHEST)
    return first - second

def cycle_counts(first_line, last_line, last_col, lines_here, cols_here):
    ext_line = first_line - OUTER + jnp.arange(lines_here + 2 * OUTER, dtype=jnp.int32)
    line_valid = ((ext_line >= 0) & (ext_line < last_line)).astype(jnp.float32)
    col_valid = (jnp.arange(cols_here, dtype=jnp.int32) < last_col).astype(jnp.float32)
    span = lines_here + 2 * OUTER
    outer_l = jnp.sum(jnp.where(window_matrix(lines_here, span, OUTER, OUTER), line_valid[None, :], 0.0), axis=1)
    guard_l = jnp.sum(jnp.where(window_matrix(lines_here, span, OUTER, GUARD), line_valid[None, :], 0.0), axis=1)
    outer_c = jnp.sum(jnp.where(window_matrix(cols_here, cols_here, 0, OUTER), col_valid[None, :], 0.0), axis=1)
    guard_c = jnp.sum(jnp.where(window_matrix(cols_here, cols_here, 0, GUARD), col_valid[None, :], 0.0), axis=1)
    return outer_l[:, None] * outer_c[None, :] - guard_l[:, None] * guard_c[None, :]

def reference(pixels, scene_lines, scene_cols):
    lines_all, cols_here, band_count = pixels.shape
    last_line = scene_lines[0]
    last_col = scene_cols[0]
    line_index = jnp.arange(lines_all, dtype=jnp.int32)
    col_index = jnp.arange(cols_here, dtype=jnp.int32)
    valid_mask = (line_index < last_line)[:, None] & (col_index < last_col)[None, :]
    masked = jnp.where(valid_mask[:, :, None], pixels, jnp.zeros((), pixels.dtype))
    pixel_total = (last_line * last_col).astype(jnp.float32)
    band_sums = jnp.sum(masked, axis=(0, 1), dtype=jnp.float32)
    spectral_mean = band_sums / pixel_total
    block_total = LINES // LINES_DEV

    def add_block(running, block_index):
        block_pixels = lax.dynamic_slice_in_dim(masked, (block_index * LINES_DEV).astype(jnp.int32), LINES_DEV, 0)
        block_valid = lax.dynamic_slice_in_dim(valid_mask, (block_index * LINES_DEV).astype(jnp.int32), LINES_DEV, 0)
        centered = jnp.where(block_valid.reshape(-1, 1), block_pixels.reshape(-1, band_count).astype(jnp.float32) - spectral_mean, 0.0)
        product = lax.dot_general(centered.astype(jnp.float32), centered.astype(jnp.float32), (((0,), (0,)), ((), ())), precision=lax.Precision.HIGHEST, preferred_element_type=jnp.float32)
        return (running + product, None)
    gram, _ = lax.scan(add_block, jnp.zeros((band_count, band_count), jnp.float32), jnp.arange(block_total, dtype=jnp.int32))
    covariance = gram / (pixel_total - 1.0)
    factor = jnp.linalg.cholesky(covariance)
    whiten = lax.linalg.triangular_solve(factor, jnp.eye(band_count, dtype=jnp.float32), left_side=True, lower=True)
    padded = jnp.pad(masked, ((OUTER, OUTER), (0, 0), (0, 0)))

    def block_score(block_index):
        first_line = (block_index * LINES_DEV).astype(jnp.int32)
        extended = lax.dynamic_slice_in_dim(padded, first_line, LINES_DEV + 2 * OUTER, 0)
        cycle_sum = cycle_part(extended, OUTER, LINES_DEV)
        counts = jnp.maximum(cycle_counts(first_line, last_line, last_col, LINES_DEV, cols_here), 1.0)
        local_mean = cycle_sum / counts[:, :, None]
        block_pixels = lax.dynamic_slice_in_dim(pixels, first_line, LINES_DEV, 0)
        deviation = (block_pixels.astype(jnp.float32) - local_mean).reshape(-1, band_count)
        whitened = lax.dot_general(deviation.astype(jnp.float32), whiten.astype(jnp.float32), (((1,), (1,)), ((), ())), precision=lax.Precision.HIGHEST, preferred_element_type=jnp.float32)
        anomaly = jnp.sum(whitened * whitened, axis=1).reshape(LINES_DEV, cols_here) / band_count
        block_valid = lax.dynamic_slice_in_dim(valid_mask, first_line, LINES_DEV, 0)
        return jnp.where(block_valid, anomaly, 0.0)
    scores = lax.map(block_score, jnp.arange(block_total, dtype=jnp.int32))
    return scores.reshape(lines_all, cols_here)
```

```python
import functools

import jax
import jax.numpy as jnp
from jax import lax
from jax.experimental import pallas as pl
from jax.experimental.pallas import tpu as pltpu
from jax.sharding import PartitionSpec as P

OUTER = 32
GUARD = 4
F32 = jnp.float32
BF16 = jnp.bfloat16
HIGH = lax.Precision.HIGHEST


def iota(shape, dim):
    return lax.broadcasted_iota(jnp.int32, shape, dim)


def gram_kernel(s_ref, x_ref, keep_ref, send_ref, acc_ref, sum_ref):
    step = pl.program_id(0)
    lines, cols, bands = x_ref.shape
    half = bands // 2
    last_line, last_col, first_line, parity = (s_ref[i] for i in range(4))
    col_mask = jnp.where(iota((cols, bands), 0) < last_col, 1.0, 0.0)
    parts = []
    for i in range(lines):
        ok = jnp.where(first_line + step * lines + i < last_line, 1.0, 0.0)
        parts.append(x_ref[i] * (col_mask * ok).astype(BF16))
    block = jnp.concatenate(parts, axis=0)
    gram = lax.dot_general(block, block, (((0,), (0,)), ((), ())), preferred_element_type=F32)
    sums = jnp.dot(jnp.ones((8, lines * cols), BF16), block, preferred_element_type=F32)

    @pl.when(step == 0)
    def _():
        acc_ref[...] = gram
        sum_ref[...] = sums

    @pl.when(step > 0)
    def _():
        acc_ref[...] += gram
        sum_ref[...] += sums

    @pl.when(step == pl.num_programs(0) - 1)
    def _():
        row = iota((half, half), 0)
        col = iota((half, half), 1)
        a22 = acc_ref[half:, half:]
        diag = jnp.sum(jnp.where(row == col, a22, 0.0), axis=0, keepdims=True)
        mixed = jnp.where(row <= col, acc_ref[:half, :half], a22)
        slot = iota((8, half), 0)
        tail = jnp.where(slot == 0, sum_ref[0:1, :half], jnp.where(slot == 1, sum_ref[0:1, half:], 0.0))
        diag = jnp.where(slot == 0, diag, 0.0)
        first = parity == 0
        cross = acc_ref[:half, half:]
        keep_ref[:half] = jnp.where(first, cross, mixed)
        send_ref[:half] = jnp.where(first, mixed, cross)
        keep_ref[half:] = jnp.where(first, tail, diag)
        send_ref[half:] = jnp.where(first, diag, tail)


def gram_parts(scalars, pixels, cols):
    lines, _, bands = pixels.shape
    half = bands // 2
    step = min(lines, 8)
    shape = jax.ShapeDtypeStruct((half + 8, half), F32)
    return pl.pallas_call(
        gram_kernel,
        out_shape=(shape, shape),
        grid_spec=pltpu.PrefetchScalarGridSpec(
            num_scalar_prefetch=1,
            grid=(lines // step,),
            in_specs=[pl.BlockSpec((step, cols, bands), lambda i, s: (i, 0, 0))],
            out_specs=[pl.BlockSpec((half + 8, half), lambda i, s: (0, 0))] * 2,
            scratch_shapes=[pltpu.VMEM((bands, bands), F32), pltpu.VMEM((8, bands), F32)],
        ),
        name="gram",
    )(scalars, pixels)


PANEL = 32


def whiten_kernel(s_ref, mine_ref, other_ref, hi_ref, lo_ref, x_ref):
    half = mine_ref.shape[1]
    bands = 2 * half
    last_line, last_col, parity = (s_ref[i] for i in (0, 1, 3))
    first = parity == 0
    total = jnp.full((1, 1), last_line * last_col, jnp.int32).astype(F32)
    cross = jnp.where(first, mine_ref[:half], other_ref[:half])
    mixed = jnp.where(first, other_ref[:half], mine_ref[:half])
    tail = jnp.where(first, mine_ref[half:], other_ref[half:])
    diag = jnp.where(first, other_ref[half:], mine_ref[half:])
    row = iota((half, half), 0)
    col = iota((half, half), 1)
    mixed_t = mixed.T
    a11 = jnp.where(row <= col, mixed, mixed_t)
    a22 = jnp.where(row > col, mixed, jnp.where(row == col, diag[0:1], mixed_t))
    sums = jnp.concatenate([tail[0:1], tail[1:2]], axis=1)
    sums = jnp.where(iota((8, bands), 0) == 0, sums, 0.0)
    outer = lax.dot_general(
        sums, sums / total, (((0,), (0,)), ((), ())), precision=HIGH, preferred_element_type=F32
    )
    scale = 1.0 / (total - 1.0)
    x_ref[:half, :half] = (a11 - outer[:half, :half]) * scale
    x_ref[:half, half:] = (cross - outer[:half, half:]) * scale
    x_ref[half:, half:] = (a22 - outer[half:, half:]) * scale
    x_ref[half:, :half] = jnp.zeros((half, half), F32)
    sub = iota((PANEL, 1), 0)
    lane = iota((PANEL, bands), 1)
    sub2 = iota((PANEL, bands), 0)
    for k in range(bands // PANEL):
        start = k * PANEL
        panel = x_ref[start : start + PANEL, :]
        norm = jnp.ones((PANEL, 1), F32)
        for j in range(PANEL):
            g = start + j
            column = panel[:, g : g + 1]
            pivot = panel[j : j + 1, g : g + 1]
            factor = jnp.where(sub > j, column * (1.0 / pivot), 0.0)
            norm = jnp.where(sub == j, lax.rsqrt(pivot), norm)
            pivot_row = jnp.where(lane[0:1] == g, 1.0, panel[j : j + 1, :])
            base = jnp.where((lane == g) & (sub2 >= j), jnp.where(sub2 == j, 1.0, 0.0), panel)
            panel = base - factor * pivot_row
        end = start + PANEL
        panel = jnp.where((lane > start + sub2) & (lane < end), 0.0, panel * norm)
        x_ref[start:end, :] = panel
        if end < bands:
            update = lax.dot_general(
                panel, panel, (((0,), (0,)), ((), ())), precision=HIGH, preferred_element_type=F32
            )
            rest = x_ref[end:, :]
            lane_r = iota((bands - end, bands), 1)
            rest = jnp.where((lane_r >= start) & (lane_r < end), 0.0, rest)
            x_ref[end:, :] = rest - update[end:, :]
    full = x_ref[...]
    whiten = jnp.where(iota((bands, bands), 1) <= iota((bands, bands), 0), full, 0.0)
    high = whiten.astype(BF16)
    hi_ref[...] = high
    lo_ref[...] = (whiten - high.astype(F32)).astype(BF16)


def whitening(scalars, mine, other):
    half = mine.shape[1]
    bands = 2 * half
    vmem = pl.BlockSpec(memory_space=pltpu.VMEM)
    shape = jax.ShapeDtypeStruct((bands, bands), BF16)
    return pl.pallas_call(
        whiten_kernel,
        out_shape=(shape, shape),
        in_specs=[pl.BlockSpec(memory_space=pltpu.SMEM), vmem, vmem],
        out_specs=(vmem, vmem),
        scratch_shapes=[pltpu.VMEM((bands, bands), F32)],
        name="whiten",
    )(scalars, mine, other)


def span(low, high):
    return jnp.maximum(high - low + 1, 0)


def score_kernel(count, role, s_ref, own_ref, sib_ref, *rest):
    nbr_refs = rest[:count]
    hi_ref, lo_ref, prior_ref, out_ref, ext_ref, acc_o, acc_g, box_ref, sems = rest[count:]
    lines = own_ref.shape[0]
    _, cols, bands = ext_ref.shape
    last_line, last_col, first_line, parity, own_role = (s_ref[i] for i in range(5))
    forward = parity == 1

    @pl.when(own_role != role)
    def _():
        out_ref[...] = prior_ref[...]

    @pl.when(own_role == role)
    def _():
        copies = [
            pltpu.make_async_copy(sib_ref, ext_ref.at[0:lines], sems.at[0]),
            pltpu.make_async_copy(own_ref.at[:, 0:cols], ext_ref.at[lines : 2 * lines], sems.at[1]),
        ]
        size = lines // count
        for k, ref in enumerate(nbr_refs):
            start = jnp.where(forward, 2 * lines + k * size, 3 * lines - (k + 1) * size)
            copies.append(pltpu.make_async_copy(ref, ext_ref.at[pl.ds(start, size)], sems.at[2 + k]))
        for copy in copies:
            copy.start()
        row = iota((cols, cols), 0)
        col = iota((cols, cols), 1)
        inside = col < last_col
        outer = jnp.where(inside & (jnp.abs(row - col) <= OUTER), 1.0, 0.0).astype(BF16)
        guard = jnp.where(inside & (jnp.abs(row - col) <= GUARD), -1.0, 0.0).astype(BF16)
        box_ref[...] = jnp.concatenate([outer, guard, outer, guard], axis=1)
        for copy in copies:
            copy.wait()

        step = jnp.where(forward, lines, -lines)
        for part, base in enumerate((first_line - step, first_line, first_line + step)):
            begin = jnp.clip(last_line - base, 0, lines)

            def clear(i, carry, part=part):
                ext_ref[part * lines + i] = jnp.zeros((cols, bands), BF16)
                return carry

            lax.fori_loop(begin, lines, clear, 0)

        def slab(j):
            within = jnp.bitwise_and(j, lines - 1)
            return j - within + jnp.where(forward, within, lines - 1 - within)

        def load(j):
            return ext_ref[slab(j)].astype(F32)

        acc_o[...] = jnp.zeros((cols, bands), F32)
        acc_g[...] = jnp.zeros((cols, bands), F32)

        def add_outer(j, carry):
            acc_o[...] += load(j)
            return carry

        def add_guard(j, carry):
            acc_g[...] += load(j)
            return carry

        lax.fori_loop(lines - OUTER, lines + OUTER, add_outer, 0)
        lax.fori_loop(lines - GUARD, lines + GUARD, add_guard, 0)
        col_id = iota((cols, 1), 0)
        outer_c = span(jnp.maximum(col_id - OUTER, 0), jnp.minimum(col_id + OUTER, last_col - 1)).astype(F32)
        guard_c = span(jnp.maximum(col_id - GUARD, 0), jnp.minimum(col_id + GUARD, last_col - 1)).astype(F32)

        def deviation(i):
            o = acc_o[...] + load(i + lines + OUTER)
            g = acc_g[...] + load(i + lines + GUARD)
            acc_o[...] = o - load(i + lines - OUTER)
            acc_g[...] = g - load(i + lines - GUARD)
            oh = o.astype(BF16)
            gh = g.astype(BF16)
            ol = (o - oh.astype(F32)).astype(BF16)
            gl = (g - gh.astype(F32)).astype(BF16)
            sums = jnp.concatenate([oh, gh, ol, gl], axis=0)
            cycle = jnp.dot(box_ref[...], sums, preferred_element_type=F32)
            line = first_line + jnp.where(forward, i, lines - 1 - i)
            outer_l = span(jnp.maximum(line - OUTER, 0), jnp.minimum(line + OUTER, last_line - 1)).astype(F32)
            guard_l = span(jnp.maximum(line - GUARD, 0), jnp.minimum(line + GUARD, last_line - 1)).astype(F32)
            counts = jnp.maximum(outer_l * outer_c - guard_l * guard_c, 1.0)
            return load(i + lines) - cycle * (1.0 / counts)

        nt = (((1,), (1,)), ((), ()))

        def pair(t, carry):
            i = 2 * t
            dev = jnp.concatenate([deviation(i), deviation(i + 1)], axis=0)
            dh = dev.astype(BF16)
            dl = (dev - dh.astype(F32)).astype(BF16)
            wh = hi_ref[...]
            white = lax.dot_general(wh, dh, nt, preferred_element_type=F32)
            white += lax.dot_general(lo_ref[...], dh, nt, preferred_element_type=F32)
            white += lax.dot_general(wh, dl, nt, preferred_element_type=F32)
            score = jnp.sum(white * white, axis=0, keepdims=True) * (1.0 / bands)
            for n in range(2):
                line = jnp.where(forward, i + n, lines - 1 - i - n)
                good = (iota((1, cols), 1) < last_col) & (first_line + line < last_line)
                out_ref[pl.ds(line, 1), 0:cols] = jnp.where(good, score[:, n * cols : (n + 1) * cols], 0.0)
            return carry

        if cols < out_ref.shape[1]:
            out_ref[...] = jnp.zeros(out_ref.shape, F32)
        lax.fori_loop(0, lines // 2, pair, 0)


def scores(scalars, own, sib, nbrs, high, low, prior, role, cols):
    lines, width, bands = own.shape
    count = len(nbrs)
    vmem = pl.BlockSpec(memory_space=pltpu.VMEM)
    hbm = pl.BlockSpec(memory_space=pl.ANY)
    return pl.pallas_call(
        functools.partial(score_kernel, count, role),
        out_shape=jax.ShapeDtypeStruct((lines, width), F32),
        in_specs=[pl.BlockSpec(memory_space=pltpu.SMEM), hbm, hbm] + [hbm] * count + [vmem] * 3,
        out_specs=vmem,
        scratch_shapes=[
            pltpu.VMEM((3 * lines, cols, bands), BF16),
            pltpu.VMEM((cols, bands), F32),
            pltpu.VMEM((cols, bands), F32),
            pltpu.VMEM((cols, 4 * cols), BF16),
            pltpu.SemaphoreType.DMA((2 + count,)),
        ],
        name="scores",
    )(scalars, own, sib, *nbrs, high, low, prior)


def body(pixels, scene_lines, scene_cols):
    lines, cols, bands = pixels.shape
    count = lax.axis_size("lines")
    index = lax.axis_index("lines")
    parity = index % 2
    role = jnp.where((index % 4 == 1) | (index % 4 == 2), 0, 1)
    scalars = jnp.stack([scene_lines[0], scene_cols[0], index * lines, parity, role]).astype(jnp.int32)
    inner = [(i, i + 1) for i in range(1, count - 1, 4)]
    cross = [(i, i + 1) for i in range(3, count - 1, 4)]
    both = lambda pairs: pairs + [(b, a) for a, b in pairs]
    swap = lambda m: [(i, i ^ m) for i in range(count)]
    send = lambda x, pairs: lax.ppermute(x, "lines", pairs)

    near = send(pixels, both(inner))
    sib = send(pixels, swap(1))
    mine, theirs = gram_parts(scalars, pixels, cols)
    mine = mine + send(theirs, swap(1))
    step = 4
    while step < count:
        mine = mine + send(mine, swap(step))
        step *= 2
    mine = mine + send(mine, swap(2))
    other = send(mine, swap(1))
    far = send(pixels, both(cross))
    high, low = whitening(scalars, mine, other)
    out = jnp.zeros((lines, cols), F32)
    out = scores(scalars, pixels, sib, [near], high, low, out, 0, cols)
    return scores(scalars, pixels, sib, [far], high, low, out, 1, cols)


def solution(mesh):
    in_specs = (P(("scene", "lines"), None, None), P("scene"), P("scene"))
    out_specs = P(("scene", "lines"), None)
    return jax.shard_map(body, mesh=mesh, in_specs=in_specs, out_specs=out_specs, check_vma=False)
```

```python
import functools

import jax
import jax.numpy as jnp
from jax import lax
from jax.experimental import pallas as pl
from jax.experimental.pallas import tpu as pltpu
from jax.sharding import PartitionSpec as P


OUTER = 32
GUARD = 4
PANEL = 32
GROUP = 4
STEP = 16
F32 = jnp.float32
BF16 = jnp.bfloat16
HIGH = lax.Precision.HIGHEST
SMEM = pl.BlockSpec(memory_space=pltpu.SMEM)
VMEM = pl.BlockSpec(memory_space=pltpu.VMEM)
HBM = pl.BlockSpec(memory_space=pl.ANY)
TN = (((0,), (0,)), ((), ()))
NT = (((1,), (1,)), ((), ()))


def iota(shape, dim):
    return lax.broadcasted_iota(jnp.int32, shape, dim)


def gram_kernel(rows_ref, cols_ref, x_ref, keep_ref, send_ref, *rest):
    *used_ref, acc_ref, sum_ref = rest
    step = pl.program_id(0)
    lines, cols, bands = x_ref.shape
    half = bands // 2
    index = lax.axis_index("lines")
    first_line = index * lines * pl.num_programs(0)
    if used_ref:
        used_ref[0][...] = x_ref[...]
    col_mask = jnp.where(iota((cols, bands), 0) < cols_ref[0], 1.0, 0.0)
    parts = []
    for i in range(lines):
        ok = jnp.where(first_line + step * lines + i < rows_ref[0], 1.0, 0.0)
        parts.append(x_ref[i] * (col_mask * ok).astype(BF16))
    block = jnp.concatenate(parts, axis=0)
    gram = lax.dot_general(block, block, TN, preferred_element_type=F32)
    sums = jnp.dot(jnp.ones((8, lines * cols), BF16), block, preferred_element_type=F32)

    @pl.when(step == 0)
    def _():
        acc_ref[...] = gram
        sum_ref[...] = sums

    @pl.when(step > 0)
    def _():
        acc_ref[...] += gram
        sum_ref[...] += sums

    @pl.when(step == pl.num_programs(0) - 1)
    def _():
        row = iota((half, half), 0)
        col = iota((half, half), 1)
        a22 = acc_ref[half:, half:]
        diag = jnp.sum(jnp.where(row == col, a22, 0.0), axis=0, keepdims=True)
        mixed = jnp.where(row <= col, acc_ref[:half, :half], a22)
        slot = iota((8, half), 0)
        tail = jnp.where(slot == 0, sum_ref[0:1, :half], jnp.where(slot == 1, sum_ref[0:1, half:], 0.0))
        diag = jnp.where(slot == 0, diag, 0.0)
        first = index % 2 == 0
        cross = acc_ref[:half, half:]
        keep_ref[:half] = jnp.where(first, cross, mixed)
        send_ref[:half] = jnp.where(first, mixed, cross)
        keep_ref[half:] = jnp.where(first, tail, diag)
        send_ref[half:] = jnp.where(first, diag, tail)


def gram_parts(rows, columns, pixels, cols):
    lines, width, bands = pixels.shape
    half = bands // 2
    step = min(lines, STEP)
    block = pl.BlockSpec((step, cols, bands), lambda i: (i, 0, 0))
    part = pl.BlockSpec((half + 8, half), lambda i: (0, 0))
    shapes = [jax.ShapeDtypeStruct((half + 8, half), F32)] * 2
    specs = [part, part]
    if cols < width:
        shapes.append(jax.ShapeDtypeStruct((lines, cols, bands), pixels.dtype))
        specs.append(block)
    return pl.pallas_call(
        gram_kernel,
        out_shape=shapes,
        grid=(lines // step,),
        in_specs=[SMEM, SMEM, block],
        out_specs=specs,
        scratch_shapes=[pltpu.VMEM((bands, bands), F32), pltpu.VMEM((8, bands), F32)],
        compiler_params=pltpu.CompilerParams(vmem_limit_bytes=16 << 20),
        name="gram",
    )(rows, columns, pixels)


def eliminate(x_ref):
    bands = x_ref.shape[0]
    half = bands // 2
    sub = iota((PANEL, half), 0)
    lane = iota((PANEL, half), 1)
    for start in range(0, bands, PANEL):
        end = start + PANEL
        side, left = divmod(start, half)
        tiles = [x_ref[start:end, :half], x_ref[start:end, half:]]
        norm = jnp.ones((PANEL, half), F32)
        columns = []
        for j in range(PANEL):
            top = j - j % 8
            columns.append(
                jnp.broadcast_to(tiles[side][top:, left + j : left + j + 1], (PANEL - top, half))
            )
        for j in range(PANEL):
            top = j - j % 8
            column = columns[j]
            pivot = column[j - top : j - top + 1, :]
            rows = sub[top:]
            factor = jnp.where(rows > j, column * (1.0 / pivot), 0.0)
            for n in range(j + 1, PANEL):
                skip = n - n % 8
                columns[n] = columns[n] - factor[skip - top :] * column[n - top : n - top + 1, :]
            norm = jnp.where(sub == j, lax.rsqrt(pivot), norm)
            for q in range(2):
                row = tiles[q][j : j + 1, :]
                base = tiles[q][top:]
                if q == side:
                    row = jnp.where(lane[0:1] == left + j, 1.0, row)
                    here = (lane[top:] == left + j) & (rows >= j)
                    base = jnp.where(here, jnp.where(rows == j, 1.0, 0.0), base)
                new = base - factor * row
                tiles[q] = new if top == 0 else jnp.concatenate([tiles[q][:top], new], axis=0)
        for q in range(2):
            value = tiles[q] * norm
            if q == side:
                value = jnp.where((lane > left + sub) & (lane < left + PANEL), 0.0, value)
            tiles[q] = value
            x_ref[start:end, q * half : (q + 1) * half] = value
        if end < bands:
            panel = jnp.concatenate(tiles, axis=1)
            skip = 0 if end < half else half
            update = lax.dot_general(panel[:, skip:], panel, TN, precision=HIGH, preferred_element_type=F32)
            lane_r = iota((bands - end, bands), 1)
            rest = jnp.where((lane_r >= start) & (lane_r < end), 0.0, x_ref[end:, :])
            x_ref[end:, :] = rest - update[end - skip :, :]


def whiten_kernel(rows_ref, cols_ref, mine_ref, other_ref, hi_ref, lo_ref, x_ref):
    half = mine_ref.shape[1]
    bands = 2 * half
    first = lax.axis_index("lines") % 2 == 0
    total = jnp.full((1, 1), rows_ref[0] * cols_ref[0], jnp.int32).astype(F32)
    cross = jnp.where(first, mine_ref[:half], other_ref[:half])
    mixed = jnp.where(first, other_ref[:half], mine_ref[:half])
    tail = jnp.where(first, mine_ref[half:], other_ref[half:])
    diag = jnp.where(first, other_ref[half:], mine_ref[half:])
    row = iota((half, half), 0)
    col = iota((half, half), 1)
    mixed_t = mixed.T
    a11 = jnp.where(row <= col, mixed, mixed_t)
    a22 = jnp.where(row > col, mixed, jnp.where(row == col, diag[0:1], mixed_t))
    sums = jnp.concatenate([tail[0:1], tail[1:2]], axis=1)
    sums = jnp.where(iota((8, bands), 0) == 0, sums, 0.0)
    outer = lax.dot_general(sums, sums / total, TN, precision=HIGH, preferred_element_type=F32)
    scale = 1.0 / (total - 1.0)
    x_ref[:half, :half] = (a11 - outer[:half, :half]) * scale
    x_ref[:half, half:] = (cross - outer[:half, half:]) * scale
    x_ref[half:, half:] = (a22 - outer[half:, half:]) * scale
    x_ref[half:, :half] = jnp.zeros((half, half), F32)
    eliminate(x_ref)
    full = x_ref[...]
    whiten = jnp.where(iota((bands, bands), 1) <= iota((bands, bands), 0), full, 0.0)
    high = whiten.astype(BF16)
    hi_ref[...] = high
    lo_ref[...] = (whiten - high.astype(F32)).astype(BF16)


def whitening(rows, columns, mine, other):
    half = mine.shape[1]
    bands = 2 * half
    shape = jax.ShapeDtypeStruct((bands, bands), BF16)
    return pl.pallas_call(
        whiten_kernel,
        out_shape=(shape, shape),
        in_specs=[SMEM, SMEM, VMEM, VMEM],
        out_specs=(VMEM, VMEM),
        scratch_shapes=[pltpu.VMEM((bands, bands), F32)],
        compiler_params=pltpu.CompilerParams(vmem_limit_bytes=8 << 20),
        name="whiten",
    )(rows, columns, mine, other)


def boxes(cols, last_col):
    row = iota((cols, cols), 0)
    col = iota((cols, cols), 1)
    inside = col < last_col
    outer = jnp.where(inside & (jnp.abs(row - col) <= OUTER), 1.0, 0.0)
    guard = jnp.where(inside & (jnp.abs(row - col) <= GUARD), 1.0, 0.0)
    return outer, guard


def slab_index(j, lines, last_line, index):
    forward = index % 2 == 1
    within = jnp.bitwise_and(j, lines - 1)
    part = (j + lines) // lines - 1
    place = jnp.where(forward, within, lines - 1 - within)
    start = (index + jnp.where(forward, part - 1, 1 - part)) * lines
    return jnp.where((j >= 0) & (start + place < last_line), part * lines + place, 3 * lines)


def begin_kernel(rows_ref, cols_ref, own_ref, sib_ref, out_ref, ext_ref, sums_ref, sems):
    lines = own_ref.shape[0]
    cols, bands = out_ref.shape
    last_line, last_col = rows_ref[0], cols_ref[0]
    index = lax.axis_index("lines")
    copies = [
        pltpu.make_async_copy(sib_ref, ext_ref.at[0:lines], sems.at[0]),
        pltpu.make_async_copy(own_ref.at[:, 0:cols], ext_ref.at[lines : 2 * lines], sems.at[1]),
    ]
    for copy in copies:
        copy.start()
    outer, guard = boxes(cols, last_col)
    box = jnp.concatenate([outer, -guard, outer, -guard], axis=1).astype(BF16)
    for copy in copies:
        copy.wait()
    other = index + jnp.where(index % 2 == 0, 1, -1)
    for part, owner in enumerate((other, index)):

        def clear(i, carry, part=part):
            ext_ref[part * lines + i] = jnp.zeros((cols, bands), BF16)
            return carry

        lax.fori_loop(jnp.clip(last_line - owner * lines, 0, lines), lines, clear, 0)
    strip = 32 if cols % 32 == 0 else 16
    near_by = [slab_index(j, lines, 1 << 30, index) for j in range(lines - GUARD - 1, lines + GUARD)]
    for r in range(0, cols, strip):

        def add(j, acc, r=r):
            return acc + ext_ref[j, r : r + strip, :].astype(F32)

        total = lax.fori_loop(0, 2 * lines, add, jnp.zeros((strip, bands), F32), unroll=16)
        close = ext_ref[near_by[0], r : r + strip, :].astype(F32)
        for place in near_by[1:]:
            close = close + ext_ref[place, r : r + strip, :].astype(F32)
        for base, value in ((0, total), (cols, close)):
            high = value.astype(BF16)
            sums_ref[base + r : base + r + strip, :] = high
            sums_ref[base + r + 2 * cols : base + r + 2 * cols + strip, :] = (value - high.astype(F32)).astype(BF16)
    out_ref[...] = jnp.dot(box, sums_ref[...], preferred_element_type=F32)


def begin(rows, columns, own, sib, cols):
    lines, _, bands = own.shape
    return pl.pallas_call(
        begin_kernel,
        out_shape=jax.ShapeDtypeStruct((cols, bands), F32),
        in_specs=[SMEM, SMEM, HBM, HBM],
        out_specs=VMEM,
        scratch_shapes=[
            pltpu.VMEM((2 * lines, cols, bands), BF16),
            pltpu.VMEM((4 * cols, bands), BF16),
            pltpu.SemaphoreType.DMA((2,)),
        ],
        compiler_params=pltpu.CompilerParams(vmem_limit_bytes=12 << 20),
        name="begin",
    )(rows, columns, own, sib)


def span(low, high):
    return jnp.maximum(high - low + 1, 0)


def score_kernel(
    rows_ref, cols_ref, own_ref, sib_ref, near_ref, far_ref, start_ref, hi_ref, lo_ref,
    out_ref, ext_ref, acc_ref, box_ref, dev_ref, w_ref, sems,
):
    lines = own_ref.shape[0]
    _, cols, bands = ext_ref.shape
    last_line, last_col = rows_ref[0], cols_ref[0]
    index = lax.axis_index("lines")
    forward = index % 2 == 1
    is_near = (index % 4 == 1) | (index % 4 == 2)
    stages = sems.shape[1]
    size = lines // stages
    group = dev_ref.shape[0] // cols

    def move(kind, s, ref=None):
        at = pl.multiple_of(jnp.where(forward, s * size, lines - (s + 1) * size), size)
        to = ext_ref.at[pl.ds(kind * lines + at, size)]
        source = (sib_ref, own_ref, ref)[kind].at[pl.ds(at, size)]
        if kind == 1:
            source = own_ref.at[pl.ds(at, size), 0:cols]
        return pltpu.make_async_copy(source, to, sems.at[kind, s])

    def launch(ref):
        move(1, 0).start()
        for s in range(stages):
            if s + 1 < stages:
                move(1, s + 1).start()
            move(0, s).start()
            move(2, s, ref).start()

    pl.when(is_near)(lambda: launch(near_ref))
    pl.when(jnp.logical_not(is_near))(lambda: launch(far_ref))
    outer, guard = boxes(cols, last_col)
    box_ref[...] = jnp.concatenate([outer, -outer, -guard, guard], axis=1).astype(BF16)
    acc_ref[...] = start_ref[...]
    w_ref[...] = jnp.concatenate([hi_ref[...], lo_ref[...], hi_ref[...]], axis=1)
    ext_ref[3 * lines] = jnp.zeros((cols, bands), BF16)
    if cols < out_ref.shape[1]:
        out_ref[...] = jnp.zeros(out_ref.shape, F32)
    col_id = iota((cols, 1), 0)
    outer_c = span(jnp.maximum(col_id - OUTER, 0), jnp.minimum(col_id + OUTER, last_col - 1)).astype(F32)
    guard_c = span(jnp.maximum(col_id - GUARD, 0), jnp.minimum(col_id + GUARD, last_col - 1)).astype(F32)

    def load(j):
        return ext_ref[slab_index(j, lines, last_line, index)]

    def deviation(i):
        own = lines + i
        moved = [load(own + OUTER), load(own - OUTER - 1), load(own + GUARD), load(own - GUARD - 1)]
        cycle = acc_ref[...] + jnp.dot(
            box_ref[...], jnp.concatenate(moved, axis=0), preferred_element_type=F32
        )
        acc_ref[...] = cycle
        place = jnp.where(forward, i, lines - 1 - i)
        line = index * lines + place
        outer_l = span(jnp.maximum(line - OUTER, 0), jnp.minimum(line + OUTER, last_line - 1)).astype(F32)
        guard_l = span(jnp.maximum(line - GUARD, 0), jnp.minimum(line + GUARD, last_line - 1)).astype(F32)
        counts = jnp.maximum(outer_l * outer_c - guard_l * guard_c, 1.0)
        return ext_ref[lines + place].astype(F32) - cycle * (1.0 / counts)

    def prepare(t):
        dev = jnp.concatenate([deviation(group * t + n) for n in range(group)], axis=0)
        high = dev.astype(BF16)
        dev_ref[:, :bands] = high
        dev_ref[:, bands:] = (dev - high.astype(F32)).astype(BF16)

    def finish(t):
        high = dev_ref[:, :bands]
        both = jnp.concatenate([high, high, dev_ref[:, bands:]], axis=1)
        white = lax.dot_general(w_ref[...], both, NT, preferred_element_type=F32)
        score = jnp.sum(white * white, axis=0, keepdims=True) * (1.0 / bands)
        for n in range(group):
            i = group * t + n
            place = jnp.where(forward, i, lines - 1 - i)
            good = (iota((1, cols), 1) < last_col) & (index * lines + place < last_line)
            out_ref[pl.ds(place, 1), 0:cols] = jnp.where(good, score[:, n * cols : (n + 1) * cols], 0.0)

    def arrive(s):
        @pl.when(s + 1 < stages)
        def _():
            move(1, s + 1).wait()

        move(0, s).wait()
        move(2, s, near_ref).wait()

    def step(t, carry):
        @pl.when(t % (size // group) == 0)
        def _():
            arrive(t // (size // group))

        finish(t - 1)
        prepare(t)
        return carry

    move(1, 0).wait()
    arrive(0)
    prepare(0)
    lax.fori_loop(1, lines // group, step, 0)
    finish(lines // group - 1)


def scores(rows, columns, own, sib, near, far, start, high, low):
    lines, width, bands = own.shape
    cols = sib.shape[1]
    stages = 4
    return pl.pallas_call(
        score_kernel,
        out_shape=jax.ShapeDtypeStruct((lines, width), F32),
        in_specs=[SMEM, SMEM, HBM, HBM, HBM, HBM, VMEM, VMEM, VMEM],
        out_specs=VMEM,
        scratch_shapes=[
            pltpu.VMEM((3 * lines + 1, cols, bands), BF16),
            pltpu.VMEM((cols, bands), F32),
            pltpu.VMEM((cols, 4 * cols), BF16),
            pltpu.VMEM((GROUP * cols, 2 * bands), BF16),
            pltpu.VMEM((bands, 3 * bands), BF16),
            pltpu.SemaphoreType.DMA((3, stages)),
        ],
        compiler_params=pltpu.CompilerParams(vmem_limit_bytes=20 << 20),
        name="scores",
    )(rows, columns, own, sib, near, far, start, high, low)


def program(cols, pixels, rows, columns):
    count = lax.axis_size("lines")
    after = lambda x, y: lax.optimization_barrier((x, y))
    swap = lambda m: [(i, i ^ m) for i in range(count)]
    both = lambda pairs: pairs + [(b, a) for a, b in pairs]

    def send(x, pairs):
        return lax.ppermute(x, "lines", pairs)

    if cols == pixels.shape[1]:
        used = pixels
        near = send(used, both([(i, i + 1) for i in range(1, count - 1, 4)]))
        mine, theirs = gram_parts(rows, columns, pixels, cols)
        mine = mine + send(theirs, swap(1))
    else:
        mine, theirs, used = gram_parts(rows, columns, pixels, cols)
        mine = mine + send(theirs, swap(1))
        used, mine = after(used, mine)
        near = send(used, both([(i, i + 1) for i in range(1, count - 1, 4)]))
    block, mine = after(used, mine)
    sib = send(block, swap(1))
    step = 4
    while step < count:
        mine = mine + send(mine, swap(step))
        step *= 2
    mine = mine + send(mine, swap(2))
    block, mine = after(used, mine)
    far = send(block, both([(i, i + 1) for i in range(3, count - 1, 4)]))
    other = send(mine, swap(1))
    start = begin(rows, columns, pixels, sib, cols)
    high, low = whitening(rows, columns, mine, other)
    return scores(rows, columns, pixels, sib, near, far, start, high, low)


def solution(mesh):
    in_specs = (P(("scene", "lines"), None, None), P("scene"), P("scene"))
    out_specs = P(("scene", "lines"), None)

    def body(pixels, rows, columns):
        width = pixels.shape[1]
        sizes = [c for c in range(64, width, 32)] + [width]
        branches = [functools.partial(program, c) for c in sizes]
        choice = sum((columns[0] > c).astype(jnp.int32) for c in sizes[:-1])
        return lax.switch(choice, branches, pixels, rows, columns)

    return jax.shard_map(body, mesh=mesh, in_specs=in_specs, out_specs=out_specs, check_vma=False)
```

```python
import functools

import jax
import jax.numpy as jnp
from jax import lax
from jax.experimental import pallas as pl
from jax.experimental.pallas import tpu as pltpu
from jax.sharding import PartitionSpec as P


OUTER = 32
GUARD = 4
PANEL = 32
GROUP = 4
STEP = 16
F32 = jnp.float32
BF16 = jnp.bfloat16
HIGH = lax.Precision.HIGHEST
SMEM = pl.BlockSpec(memory_space=pltpu.SMEM)
VMEM = pl.BlockSpec(memory_space=pltpu.VMEM)
HBM = pl.BlockSpec(memory_space=pl.ANY)
TN = (((0,), (0,)), ((), ()))
NT = (((1,), (1,)), ((), ()))


def iota(shape, dim):
    return lax.broadcasted_iota(jnp.int32, shape, dim)


def gram_kernel(rows_ref, cols_ref, x_ref, keep_ref, send_ref, *rest):
    *used_ref, acc_ref, sum_ref = rest
    step = pl.program_id(0)
    lines, cols, bands = x_ref.shape
    half = bands // 2
    index = lax.axis_index("lines")
    first_line = index * lines * pl.num_programs(0)
    if used_ref:
        used_ref[0][...] = x_ref[...]
    col_mask = jnp.where(iota((cols, bands), 0) < cols_ref[0], 1.0, 0.0)
    parts = []
    for i in range(lines):
        ok = jnp.where(first_line + step * lines + i < rows_ref[0], 1.0, 0.0)
        parts.append(x_ref[i] * (col_mask * ok).astype(BF16))
    block = jnp.concatenate(parts, axis=0)
    gram = lax.dot_general(block, block, TN, preferred_element_type=F32)
    sums = jnp.dot(jnp.ones((8, lines * cols), BF16), block, preferred_element_type=F32)

    @pl.when(step == 0)
    def _():
        acc_ref[...] = gram
        sum_ref[...] = sums

    @pl.when(step > 0)
    def _():
        acc_ref[...] += gram
        sum_ref[...] += sums

    @pl.when(step == pl.num_programs(0) - 1)
    def _():
        row = iota((half, half), 0)
        col = iota((half, half), 1)
        a22 = acc_ref[half:, half:]
        diag = jnp.sum(jnp.where(row == col, a22, 0.0), axis=0, keepdims=True)
        mixed = jnp.where(row <= col, acc_ref[:half, :half], a22)
        slot = iota((8, half), 0)
        tail = jnp.where(slot == 0, sum_ref[0:1, :half], jnp.where(slot == 1, sum_ref[0:1, half:], 0.0))
        diag = jnp.where(slot == 0, diag, 0.0)
        first = index % 2 == 0
        cross = acc_ref[:half, half:]
        keep_ref[:half] = jnp.where(first, cross, mixed)
        send_ref[:half] = jnp.where(first, mixed, cross)
        keep_ref[half:] = jnp.where(first, tail, diag)
        send_ref[half:] = jnp.where(first, diag, tail)


def gram_parts(rows, columns, pixels, cols):
    lines, width, bands = pixels.shape
    half = bands // 2
    step = min(lines, STEP)
    block = pl.BlockSpec((step, cols, bands), lambda i: (i, 0, 0))
    part = pl.BlockSpec((half + 8, half), lambda i: (0, 0))
    shapes = [jax.ShapeDtypeStruct((half + 8, half), F32)] * 2
    specs = [part, part]
    if cols < width:
        shapes.append(jax.ShapeDtypeStruct((lines, cols, bands), pixels.dtype))
        specs.append(block)
    return pl.pallas_call(
        gram_kernel,
        out_shape=shapes,
        grid=(lines // step,),
        in_specs=[SMEM, SMEM, block],
        out_specs=specs,
        scratch_shapes=[pltpu.VMEM((bands, bands), F32), pltpu.VMEM((8, bands), F32)],
        compiler_params=pltpu.CompilerParams(vmem_limit_bytes=16 << 20),
        name="gram",
    )(rows, columns, pixels)


def eliminate(x_ref):
    half = x_ref.shape[0] // 2
    sub = iota((PANEL, half), 0)
    lane = iota((PANEL, half), 1)

    def side_pass(side, carry):
        base = pl.multiple_of(side * half, half)
        away = pl.multiple_of((1 - side) * half, half)
        both = (pl.ds(base, half), pl.ds(away, half))
        for left in range(0, half, PANEL):
            rows_at = pl.ds(pl.multiple_of(base + left, PANEL), PANEL)
            tiles = [x_ref[rows_at, at] for at in both]
            norm = jnp.ones((PANEL, half), F32)
            columns = []
            for j in range(PANEL):
                top = j - j % 8
                columns.append(jnp.broadcast_to(tiles[0][top:, left + j : left + j + 1], (PANEL - top, half)))
            for j in range(PANEL):
                top = j - j % 8
                column = columns[j]
                pivot = column[j - top : j - top + 1, :]
                rows = sub[top:]
                factor = jnp.where(rows > j, column * (1.0 / pivot), 0.0)
                for n in range(j + 1, PANEL):
                    skip = n - n % 8
                    columns[n] = columns[n] - factor[skip - top :] * column[n - top : n - top + 1, :]
                norm = jnp.where(sub == j, lax.rsqrt(pivot), norm)
                for q in range(2):
                    row = tiles[q][j : j + 1, :]
                    old = tiles[q][top:]
                    if q == 0:
                        row = jnp.where(lane[0:1] == left + j, 1.0, row)
                        here = (lane[top:] == left + j) & (rows >= j)
                        old = jnp.where(here, jnp.where(rows == j, 1.0, 0.0), old)
                    new = old - factor * row
                    tiles[q] = new if top == 0 else jnp.concatenate([tiles[q][:top], new], axis=0)
            tiles = [tile * norm for tile in tiles]
            tiles[0] = jnp.where((lane > left + sub) & (lane < left + PANEL), 0.0, tiles[0])
            for tile, at in zip(tiles, both):
                x_ref[rows_at, at] = tile
            panel = jnp.concatenate(tiles, axis=1)
            end = left + PANEL
            lane_r = iota((half, half), 1)
            block = (lane_r >= left) & (lane_r < end)
            if end < half:
                update = lax.dot_general(tiles[0], panel, TN, precision=HIGH, preferred_element_type=F32)
                rest_at = pl.ds(pl.multiple_of(base + end, PANEL), half - end)
                rest = jnp.where(block[end:], 0.0, x_ref[rest_at, both[0]])
                x_ref[rest_at, both[0]] = rest - update[end:, :half]
                x_ref[rest_at, both[1]] = x_ref[rest_at, both[1]] - update[end:, half:]
            update = lax.dot_general(tiles[1], panel, TN, precision=HIGH, preferred_element_type=F32)
            below = side == 0
            for q in range(2):
                old = x_ref[both[1], both[q]]
                new = (jnp.where(block, 0.0, old) if q == 0 else old) - update[:, q * half : (q + 1) * half]
                x_ref[both[1], both[q]] = jnp.where(below, new, old)
        return carry

    lax.fori_loop(0, 2, side_pass, 0)


def whiten_kernel(rows_ref, cols_ref, mine_ref, other_ref, hi_ref, lo_ref, x_ref):
    half = mine_ref.shape[1]
    bands = 2 * half
    first = lax.axis_index("lines") % 2 == 0
    total = jnp.full((1, 1), rows_ref[0] * cols_ref[0], jnp.int32).astype(F32)
    cross = jnp.where(first, mine_ref[:half], other_ref[:half])
    mixed = jnp.where(first, other_ref[:half], mine_ref[:half])
    tail = jnp.where(first, mine_ref[half:], other_ref[half:])
    diag = jnp.where(first, other_ref[half:], mine_ref[half:])
    row = iota((half, half), 0)
    col = iota((half, half), 1)
    mixed_t = mixed.T
    a11 = jnp.where(row <= col, mixed, mixed_t)
    a22 = jnp.where(row > col, mixed, jnp.where(row == col, diag[0:1], mixed_t))
    sums = jnp.concatenate([tail[0:1], tail[1:2]], axis=1)
    sums = jnp.where(iota((8, bands), 0) == 0, sums, 0.0)
    outer = lax.dot_general(sums, sums / total, TN, precision=HIGH, preferred_element_type=F32)
    scale = 1.0 / (total - 1.0)
    x_ref[:half, :half] = (a11 - outer[:half, :half]) * scale
    x_ref[:half, half:] = (cross - outer[:half, half:]) * scale
    x_ref[half:, half:] = (a22 - outer[half:, half:]) * scale
    x_ref[half:, :half] = jnp.zeros((half, half), F32)
    eliminate(x_ref)
    full = x_ref[...]
    whiten = jnp.where(iota((bands, bands), 1) <= iota((bands, bands), 0), full, 0.0)
    high = whiten.astype(BF16)
    hi_ref[...] = high
    lo_ref[...] = (whiten - high.astype(F32)).astype(BF16)


def whitening(rows, columns, mine, other):
    half = mine.shape[1]
    bands = 2 * half
    shape = jax.ShapeDtypeStruct((bands, bands), BF16)
    return pl.pallas_call(
        whiten_kernel,
        out_shape=(shape, shape),
        in_specs=[SMEM, SMEM, VMEM, VMEM],
        out_specs=(VMEM, VMEM),
        scratch_shapes=[pltpu.VMEM((bands, bands), F32)],
        compiler_params=pltpu.CompilerParams(vmem_limit_bytes=8 << 20),
        name="whiten",
    )(rows, columns, mine, other)


def boxes(cols, last_col):
    row = iota((cols, cols), 0)
    col = iota((cols, cols), 1)
    inside = col < last_col
    outer = jnp.where(inside & (jnp.abs(row - col) <= OUTER), 1.0, 0.0)
    guard = jnp.where(inside & (jnp.abs(row - col) <= GUARD), 1.0, 0.0)
    return outer, guard


def slab_index(j, lines, last_line, index):
    forward = index % 2 == 1
    within = jnp.bitwise_and(j, lines - 1)
    part = (j + lines) // lines - 1
    place = jnp.where(forward, within, lines - 1 - within)
    start = (index + jnp.where(forward, part - 1, 1 - part)) * lines
    return jnp.where((j >= 0) & (start + place < last_line), part * lines + place, 3 * lines)


def begin_kernel(rows_ref, cols_ref, own_ref, sib_ref, out_ref, ext_ref, sums_ref, sems):
    lines = own_ref.shape[0]
    cols, bands = out_ref.shape
    last_line, last_col = rows_ref[0], cols_ref[0]
    index = lax.axis_index("lines")
    copies = [
        pltpu.make_async_copy(sib_ref, ext_ref.at[0:lines], sems.at[0]),
        pltpu.make_async_copy(own_ref.at[:, 0:cols], ext_ref.at[lines : 2 * lines], sems.at[1]),
    ]
    for copy in copies:
        copy.start()
    outer, guard = boxes(cols, last_col)
    box = jnp.concatenate([outer, -guard, outer, -guard], axis=1).astype(BF16)
    for copy in copies:
        copy.wait()
    other = index + jnp.where(index % 2 == 0, 1, -1)
    for part, owner in enumerate((other, index)):

        def clear(i, carry, part=part):
            ext_ref[part * lines + i] = jnp.zeros((cols, bands), BF16)
            return carry

        lax.fori_loop(jnp.clip(last_line - owner * lines, 0, lines), lines, clear, 0)
    strip = 32 if cols % 32 == 0 else 16
    near_by = [slab_index(j, lines, 1 << 30, index) for j in range(lines - GUARD - 1, lines + GUARD)]
    for r in range(0, cols, strip):

        def add(j, acc, r=r):
            return acc + ext_ref[j, r : r + strip, :].astype(F32)

        total = lax.fori_loop(0, 2 * lines, add, jnp.zeros((strip, bands), F32), unroll=16)
        close = ext_ref[near_by[0], r : r + strip, :].astype(F32)
        for place in near_by[1:]:
            close = close + ext_ref[place, r : r + strip, :].astype(F32)
        for base, value in ((0, total), (cols, close)):
            high = value.astype(BF16)
            sums_ref[base + r : base + r + strip, :] = high
            sums_ref[base + r + 2 * cols : base + r + 2 * cols + strip, :] = (value - high.astype(F32)).astype(BF16)
    out_ref[...] = jnp.dot(box, sums_ref[...], preferred_element_type=F32)


def begin(rows, columns, own, sib, cols):
    lines, _, bands = own.shape
    return pl.pallas_call(
        begin_kernel,
        out_shape=jax.ShapeDtypeStruct((cols, bands), F32),
        in_specs=[SMEM, SMEM, HBM, HBM],
        out_specs=VMEM,
        scratch_shapes=[
            pltpu.VMEM((2 * lines, cols, bands), BF16),
            pltpu.VMEM((4 * cols, bands), BF16),
            pltpu.SemaphoreType.DMA((2,)),
        ],
        compiler_params=pltpu.CompilerParams(vmem_limit_bytes=12 << 20),
        name="begin",
    )(rows, columns, own, sib)


def span(low, high):
    return jnp.maximum(high - low + 1, 0)


def score_kernel(
    rows_ref, cols_ref, own_ref, sib_ref, near_ref, far_ref, start_ref, hi_ref, lo_ref,
    out_ref, ext_ref, acc_ref, box_ref, dev_ref, w_ref, sems,
):
    lines = own_ref.shape[0]
    _, cols, bands = ext_ref.shape
    last_line, last_col = rows_ref[0], cols_ref[0]
    index = lax.axis_index("lines")
    forward = index % 2 == 1
    is_near = (index % 4 == 1) | (index % 4 == 2)
    stages = sems.shape[1]
    size = lines // stages
    group = dev_ref.shape[0] // cols

    def move(kind, s, ref=None):
        at = pl.multiple_of(jnp.where(forward, s * size, lines - (s + 1) * size), size)
        to = ext_ref.at[pl.ds(kind * lines + at, size)]
        source = (sib_ref, own_ref, ref)[kind].at[pl.ds(at, size)]
        if kind == 1:
            source = own_ref.at[pl.ds(at, size), 0:cols]
        return pltpu.make_async_copy(source, to, sems.at[kind, s])

    def launch(ref):
        move(1, 0).start()
        for s in range(stages):
            if s + 1 < stages:
                move(1, s + 1).start()
            move(0, s).start()
            move(2, s, ref).start()

    pl.when(is_near)(lambda: launch(near_ref))
    pl.when(jnp.logical_not(is_near))(lambda: launch(far_ref))
    outer, guard = boxes(cols, last_col)
    box_ref[...] = jnp.concatenate([outer, -outer, -guard, guard], axis=1).astype(BF16)
    acc_ref[...] = start_ref[...]
    w_ref[...] = jnp.concatenate([hi_ref[...], lo_ref[...], hi_ref[...]], axis=1)
    ext_ref[3 * lines] = jnp.zeros((cols, bands), BF16)
    if cols < out_ref.shape[1]:
        out_ref[...] = jnp.zeros(out_ref.shape, F32)
    col_id = iota((cols, 1), 0)
    outer_c = span(jnp.maximum(col_id - OUTER, 0), jnp.minimum(col_id + OUTER, last_col - 1)).astype(F32)
    guard_c = span(jnp.maximum(col_id - GUARD, 0), jnp.minimum(col_id + GUARD, last_col - 1)).astype(F32)

    def load(j):
        return ext_ref[slab_index(j, lines, last_line, index)]

    def deviation(i):
        own = lines + i
        moved = [load(own + OUTER), load(own - OUTER - 1), load(own + GUARD), load(own - GUARD - 1)]
        cycle = acc_ref[...] + jnp.dot(
            box_ref[...], jnp.concatenate(moved, axis=0), preferred_element_type=F32
        )
        acc_ref[...] = cycle
        place = jnp.where(forward, i, lines - 1 - i)
        line = index * lines + place
        outer_l = span(jnp.maximum(line - OUTER, 0), jnp.minimum(line + OUTER, last_line - 1)).astype(F32)
        guard_l = span(jnp.maximum(line - GUARD, 0), jnp.minimum(line + GUARD, last_line - 1)).astype(F32)
        counts = jnp.maximum(outer_l * outer_c - guard_l * guard_c, 1.0)
        return ext_ref[lines + place].astype(F32) - cycle * (1.0 / counts)

    def prepare(t):
        dev = jnp.concatenate([deviation(group * t + n) for n in range(group)], axis=0)
        high = dev.astype(BF16)
        dev_ref[:, :bands] = high
        dev_ref[:, bands:] = (dev - high.astype(F32)).astype(BF16)

    def finish(t):
        high = dev_ref[:, :bands]
        both = jnp.concatenate([high, high, dev_ref[:, bands:]], axis=1)
        white = lax.dot_general(w_ref[...], both, NT, preferred_element_type=F32)
        score = jnp.sum(white * white, axis=0, keepdims=True) * (1.0 / bands)
        for n in range(group):
            i = jnp.maximum(group * t + n, 0)
            place = jnp.where(forward, i, lines - 1 - i)
            good = (iota((1, cols), 1) < last_col) & (index * lines + place < last_line)
            out_ref[pl.ds(place, 1), 0:cols] = jnp.where(good, score[:, n * cols : (n + 1) * cols], 0.0)

    def arrive(s):
        @pl.when(s + 1 < stages)
        def _():
            move(1, s + 1).wait()

        move(0, s).wait()
        move(2, s, near_ref).wait()

    last = lines // group - 1

    def step(t, carry):
        @pl.when((t % (size // group) == 0) & (t <= last))
        def _():
            arrive(t // (size // group))

        finish(t - 1)
        prepare(jnp.minimum(t, last))
        return carry

    dev_ref[...] = jnp.zeros(dev_ref.shape, BF16)
    move(1, 0).wait()
    lax.fori_loop(0, last + 2, step, 0)


def scores(rows, columns, own, sib, near, far, start, high, low):
    lines, width, bands = own.shape
    cols = sib.shape[1]
    stages = 2
    return pl.pallas_call(
        score_kernel,
        out_shape=jax.ShapeDtypeStruct((lines, width), F32),
        in_specs=[SMEM, SMEM, HBM, HBM, HBM, HBM, VMEM, VMEM, VMEM],
        out_specs=VMEM,
        scratch_shapes=[
            pltpu.VMEM((3 * lines + 1, cols, bands), BF16),
            pltpu.VMEM((cols, bands), F32),
            pltpu.VMEM((cols, 4 * cols), BF16),
            pltpu.VMEM((GROUP * cols, 2 * bands), BF16),
            pltpu.VMEM((bands, 3 * bands), BF16),
            pltpu.SemaphoreType.DMA((3, stages)),
        ],
        compiler_params=pltpu.CompilerParams(vmem_limit_bytes=20 << 20),
        name="scores",
    )(rows, columns, own, sib, near, far, start, high, low)


def program(cols, pixels, rows, columns):
    count = lax.axis_size("lines")
    after = lambda x, y: lax.optimization_barrier((x, y))
    swap = lambda m: [(i, i ^ m) for i in range(count)]
    both = lambda pairs: pairs + [(b, a) for a, b in pairs]

    def send(x, pairs):
        return lax.ppermute(x, "lines", pairs)

    if cols == pixels.shape[1]:
        used = pixels
        mine, theirs = gram_parts(rows, columns, pixels, cols)
    else:
        mine, theirs, used = gram_parts(rows, columns, pixels, cols)
    mine = mine + send(theirs, swap(1))
    used, mine = after(used, mine)
    sib = send(used, swap(1))
    near = send(used, both([(i, i + 1) for i in range(1, count - 1, 4)]))
    mine = mine + send(mine, swap(2))
    step = 4
    while 2 * step < count:
        mine = mine + send(mine, swap(step))
        step *= 2
    block, mine = after(used, mine)
    mine = mine + send(mine, swap(step))
    far = send(block, both([(i, i + 1) for i in range(3, count - 1, 4)]))
    other = send(mine, swap(1))
    start = begin(rows, columns, pixels, sib, cols)
    high, low = whitening(rows, columns, mine, other)
    return scores(rows, columns, pixels, sib, near, far, start, high, low)


def solution(mesh):
    in_specs = (P(("scene", "lines"), None, None), P("scene"), P("scene"))
    out_specs = P(("scene", "lines"), None)

    def body(pixels, rows, columns):
        width = pixels.shape[1]
        sizes = [c for c in range(64, width, 16)] + [width]
        branches = [functools.partial(program, c) for c in sizes]
        choice = sum((columns[0] > c).astype(jnp.int32) for c in sizes[:-1])
        return lax.switch(choice, branches, pixels, rows, columns)

    return jax.shard_map(body, mesh=mesh, in_specs=in_specs, out_specs=out_specs, check_vma=False)
```

```python
import functools

import jax
import jax.numpy as jnp
from jax import lax
from jax.experimental import pallas as pl
from jax.experimental.pallas import tpu as pltpu
from jax.sharding import PartitionSpec as P


OUTER = 32
GUARD = 4
PANEL = 32
GROUP = 4
STEP = 16
F32 = jnp.float32
BF16 = jnp.bfloat16
HIGH = lax.Precision.HIGHEST
SMEM = pl.BlockSpec(memory_space=pltpu.SMEM)
VMEM = pl.BlockSpec(memory_space=pltpu.VMEM)
HBM = pl.BlockSpec(memory_space=pl.ANY)
TN = (((0,), (0,)), ((), ()))
NT = (((1,), (1,)), ((), ()))


def iota(shape, dim):
    return lax.broadcasted_iota(jnp.int32, shape, dim)


def gram_kernel(rows_ref, cols_ref, x_ref, keep_ref, send_ref, *rest):
    *used_ref, acc_ref, sum_ref = rest
    step = pl.program_id(0)
    lines, cols, bands = x_ref.shape
    half = bands // 2
    index = lax.axis_index("lines")
    first_line = index * lines * pl.num_programs(0)
    if used_ref:
        used_ref[0][...] = x_ref[...]
    col_mask = jnp.where(iota((cols, bands), 0) < cols_ref[0], 1.0, 0.0)
    parts = []
    for i in range(lines):
        ok = jnp.where(first_line + step * lines + i < rows_ref[0], 1.0, 0.0)
        parts.append(x_ref[i] * (col_mask * ok).astype(BF16))
    block = jnp.concatenate(parts, axis=0)
    gram = lax.dot_general(block, block, TN, preferred_element_type=F32)
    sums = jnp.dot(jnp.ones((8, lines * cols), BF16), block, preferred_element_type=F32)

    @pl.when(step == 0)
    def _():
        acc_ref[...] = gram
        sum_ref[...] = sums

    @pl.when(step > 0)
    def _():
        acc_ref[...] += gram
        sum_ref[...] += sums

    @pl.when(step == pl.num_programs(0) - 1)
    def _():
        row = iota((half, half), 0)
        col = iota((half, half), 1)
        a22 = acc_ref[half:, half:]
        diag = jnp.sum(jnp.where(row == col, a22, 0.0), axis=0, keepdims=True)
        mixed = jnp.where(row <= col, acc_ref[:half, :half], a22)
        slot = iota((8, half), 0)
        tail = jnp.where(slot == 0, sum_ref[0:1, :half], jnp.where(slot == 1, sum_ref[0:1, half:], 0.0))
        diag = jnp.where(slot == 0, diag, 0.0)
        first = index % 2 == 0
        cross = acc_ref[:half, half:]
        keep_ref[:half] = jnp.where(first, cross, mixed)
        send_ref[:half] = jnp.where(first, mixed, cross)
        keep_ref[half:] = jnp.where(first, tail, diag)
        send_ref[half:] = jnp.where(first, diag, tail)


def gram_parts(rows, columns, pixels, cols):
    lines, width, bands = pixels.shape
    half = bands // 2
    step = min(lines, STEP)
    block = pl.BlockSpec((step, cols, bands), lambda i: (i, 0, 0))
    part = pl.BlockSpec((half + 8, half), lambda i: (0, 0))
    shapes = [jax.ShapeDtypeStruct((half + 8, half), F32)] * 2
    specs = [part, part]
    if cols < width:
        shapes.append(jax.ShapeDtypeStruct((lines, cols, bands), pixels.dtype))
        specs.append(block)
    return pl.pallas_call(
        gram_kernel,
        out_shape=shapes,
        grid=(lines // step,),
        in_specs=[SMEM, SMEM, block],
        out_specs=specs,
        scratch_shapes=[pltpu.VMEM((bands, bands), F32), pltpu.VMEM((8, bands), F32)],
        compiler_params=pltpu.CompilerParams(vmem_limit_bytes=16 << 20),
        name="gram",
    )(rows, columns, pixels)


def halves_kernel(x_ref, first_ref, rest_ref, sems):
    size, cols, _ = first_ref.shape
    odd = lax.axis_index("lines") % 2
    copies = []
    for n, ref in enumerate((first_ref, rest_ref)):
        at = pl.multiple_of(jnp.where(odd == n, 0, 1) * size, size)
        copies.append(pltpu.make_async_copy(x_ref.at[pl.ds(at, size), 0:cols], ref, sems.at[n]))
    for copy in copies:
        copy.start()
    for copy in copies:
        copy.wait()


def halves(pixels, cols):
    lines, _, bands = pixels.shape
    shape = jax.ShapeDtypeStruct((lines // 2, cols, bands), pixels.dtype)
    return pl.pallas_call(
        halves_kernel,
        out_shape=(shape, shape),
        in_specs=[HBM],
        out_specs=(VMEM, VMEM),
        scratch_shapes=[pltpu.SemaphoreType.DMA((2,))],
        compiler_params=pltpu.CompilerParams(vmem_limit_bytes=8 << 20),
        name="halves",
    )(pixels)


def eliminate(x_ref):
    half = x_ref.shape[0] // 2
    sub = iota((PANEL, half), 0)
    lane = iota((PANEL, half), 1)

    def side_pass(side, carry):
        base = pl.multiple_of(side * half, half)
        away = pl.multiple_of((1 - side) * half, half)
        both = (pl.ds(base, half), pl.ds(away, half))
        for left in range(0, half, PANEL):
            rows_at = pl.ds(pl.multiple_of(base + left, PANEL), PANEL)
            tiles = [x_ref[rows_at, at] for at in both]
            norm = jnp.ones((PANEL, half), F32)
            columns = []
            for j in range(PANEL):
                top = j - j % 8
                columns.append(jnp.broadcast_to(tiles[0][top:, left + j : left + j + 1], (PANEL - top, half)))
            for j in range(PANEL):
                top = j - j % 8
                column = columns[j]
                pivot = column[j - top : j - top + 1, :]
                rows = sub[top:]
                factor = jnp.where(rows > j, column * (1.0 / pivot), 0.0)
                for n in range(j + 1, PANEL):
                    skip = n - n % 8
                    columns[n] = columns[n] - factor[skip - top :] * column[n - top : n - top + 1, :]
                norm = jnp.where(sub == j, lax.rsqrt(pivot), norm)
                for q in range(2):
                    row = tiles[q][j : j + 1, :]
                    old = tiles[q][top:]
                    if q == 0:
                        row = jnp.where(lane[0:1] == left + j, 1.0, row)
                        here = (lane[top:] == left + j) & (rows >= j)
                        old = jnp.where(here, jnp.where(rows == j, 1.0, 0.0), old)
                    new = old - factor * row
                    tiles[q] = new if top == 0 else jnp.concatenate([tiles[q][:top], new], axis=0)
            tiles = [tile * norm for tile in tiles]
            tiles[0] = jnp.where((lane > left + sub) & (lane < left + PANEL), 0.0, tiles[0])
            for tile, at in zip(tiles, both):
                x_ref[rows_at, at] = tile
            panel = jnp.concatenate(tiles, axis=1)
            end = left + PANEL
            lane_r = iota((half, half), 1)
            block = (lane_r >= left) & (lane_r < end)
            if end < half:
                update = lax.dot_general(tiles[0], panel, TN, precision=HIGH, preferred_element_type=F32)
                rest_at = pl.ds(pl.multiple_of(base + end, PANEL), half - end)
                rest = jnp.where(block[end:], 0.0, x_ref[rest_at, both[0]])
                x_ref[rest_at, both[0]] = rest - update[end:, :half]
                x_ref[rest_at, both[1]] = x_ref[rest_at, both[1]] - update[end:, half:]
            update = lax.dot_general(tiles[1], panel, TN, precision=HIGH, preferred_element_type=F32)
            below = side == 0
            for q in range(2):
                old = x_ref[both[1], both[q]]
                new = (jnp.where(block, 0.0, old) if q == 0 else old) - update[:, q * half : (q + 1) * half]
                x_ref[both[1], both[q]] = jnp.where(below, new, old)
        return carry

    lax.fori_loop(0, 2, side_pass, 0)


def whiten_kernel(rows_ref, cols_ref, mine_ref, other_ref, hi_ref, lo_ref, x_ref):
    half = mine_ref.shape[1]
    bands = 2 * half
    first = lax.axis_index("lines") % 2 == 0
    total = jnp.full((1, 1), rows_ref[0] * cols_ref[0], jnp.int32).astype(F32)
    cross = jnp.where(first, mine_ref[:half], other_ref[:half])
    mixed = jnp.where(first, other_ref[:half], mine_ref[:half])
    tail = jnp.where(first, mine_ref[half:], other_ref[half:])
    diag = jnp.where(first, other_ref[half:], mine_ref[half:])
    row = iota((half, half), 0)
    col = iota((half, half), 1)
    mixed_t = mixed.T
    a11 = jnp.where(row <= col, mixed, mixed_t)
    a22 = jnp.where(row > col, mixed, jnp.where(row == col, diag[0:1], mixed_t))
    sums = jnp.concatenate([tail[0:1], tail[1:2]], axis=1)
    sums = jnp.where(iota((8, bands), 0) == 0, sums, 0.0)
    outer = lax.dot_general(sums, sums / total, TN, precision=HIGH, preferred_element_type=F32)
    scale = 1.0 / (total - 1.0)
    x_ref[:half, :half] = (a11 - outer[:half, :half]) * scale
    x_ref[:half, half:] = (cross - outer[:half, half:]) * scale
    x_ref[half:, half:] = (a22 - outer[half:, half:]) * scale
    x_ref[half:, :half] = jnp.zeros((half, half), F32)
    eliminate(x_ref)
    full = x_ref[...]
    whiten = jnp.where(iota((bands, bands), 1) <= iota((bands, bands), 0), full, 0.0)
    high = whiten.astype(BF16)
    hi_ref[...] = high
    lo_ref[...] = (whiten - high.astype(F32)).astype(BF16)


def whitening(rows, columns, mine, other):
    half = mine.shape[1]
    bands = 2 * half
    shape = jax.ShapeDtypeStruct((bands, bands), BF16)
    return pl.pallas_call(
        whiten_kernel,
        out_shape=(shape, shape),
        in_specs=[SMEM, SMEM, VMEM, VMEM],
        out_specs=(VMEM, VMEM),
        scratch_shapes=[pltpu.VMEM((bands, bands), F32)],
        compiler_params=pltpu.CompilerParams(vmem_limit_bytes=8 << 20),
        name="whiten",
    )(rows, columns, mine, other)


def boxes(cols, last_col):
    row = iota((cols, cols), 0)
    col = iota((cols, cols), 1)
    inside = col < last_col
    outer = jnp.where(inside & (jnp.abs(row - col) <= OUTER), 1.0, 0.0)
    guard = jnp.where(inside & (jnp.abs(row - col) <= GUARD), 1.0, 0.0)
    return outer, guard


def slab_index(j, lines, last_line, index):
    forward = index % 2 == 1
    within = jnp.bitwise_and(j, lines - 1)
    part = (j + lines) // lines - 1
    place = jnp.where(forward, within, lines - 1 - within)
    start = (index + jnp.where(forward, part - 1, 1 - part)) * lines
    return jnp.where((j >= 0) & (start + place < last_line), part * lines + place, 3 * lines)


def begin_kernel(rows_ref, cols_ref, own_ref, sib_ref, out_ref, ext_ref, sums_ref, sems):
    lines = own_ref.shape[0]
    cols, bands = out_ref.shape
    last_line, last_col = rows_ref[0], cols_ref[0]
    index = lax.axis_index("lines")
    copies = [
        pltpu.make_async_copy(sib_ref, ext_ref.at[0:lines], sems.at[0]),
        pltpu.make_async_copy(own_ref.at[:, 0:cols], ext_ref.at[lines : 2 * lines], sems.at[1]),
    ]
    for copy in copies:
        copy.start()
    outer, guard = boxes(cols, last_col)
    box = jnp.concatenate([outer, -guard, outer, -guard], axis=1).astype(BF16)
    for copy in copies:
        copy.wait()
    other = index + jnp.where(index % 2 == 0, 1, -1)
    for part, owner in enumerate((other, index)):

        def clear(i, carry, part=part):
            ext_ref[part * lines + i] = jnp.zeros((cols, bands), BF16)
            return carry

        lax.fori_loop(jnp.clip(last_line - owner * lines, 0, lines), lines, clear, 0)
    strip = 32 if cols % 32 == 0 else 16
    near_by = [slab_index(j, lines, 1 << 30, index) for j in range(lines - GUARD - 1, lines + GUARD)]
    for r in range(0, cols, strip):

        def add(j, acc, r=r):
            return acc + ext_ref[j, r : r + strip, :].astype(F32)

        total = lax.fori_loop(0, 2 * lines, add, jnp.zeros((strip, bands), F32), unroll=16)
        close = ext_ref[near_by[0], r : r + strip, :].astype(F32)
        for place in near_by[1:]:
            close = close + ext_ref[place, r : r + strip, :].astype(F32)
        for base, value in ((0, total), (cols, close)):
            high = value.astype(BF16)
            sums_ref[base + r : base + r + strip, :] = high
            sums_ref[base + r + 2 * cols : base + r + 2 * cols + strip, :] = (value - high.astype(F32)).astype(BF16)
    out_ref[...] = jnp.dot(box, sums_ref[...], preferred_element_type=F32)


def begin(rows, columns, own, sib, cols):
    lines, _, bands = own.shape
    return pl.pallas_call(
        begin_kernel,
        out_shape=jax.ShapeDtypeStruct((cols, bands), F32),
        in_specs=[SMEM, SMEM, HBM, HBM],
        out_specs=VMEM,
        scratch_shapes=[
            pltpu.VMEM((2 * lines, cols, bands), BF16),
            pltpu.VMEM((4 * cols, bands), BF16),
            pltpu.SemaphoreType.DMA((2,)),
        ],
        compiler_params=pltpu.CompilerParams(vmem_limit_bytes=12 << 20),
        name="begin",
    )(rows, columns, own, sib)


def span(low, high):
    return jnp.maximum(high - low + 1, 0)


def score_kernel(
    near_refs, rows_ref, cols_ref, own_ref, sib_ref, far_ref, start_ref, hi_ref, lo_ref,
    out_ref, ext_ref, acc_ref, box_ref, dev_ref, w_ref, sems,
):
    lines = own_ref.shape[0]
    _, cols, bands = ext_ref.shape
    last_line, last_col = rows_ref[0], cols_ref[0]
    index = lax.axis_index("lines")
    forward = index % 2 == 1
    is_near = (index % 4 == 1) | (index % 4 == 2)
    group = dev_ref.shape[0] // cols

    early = lines // 2
    pieces = ((1, 0, lines), (2, 0, early), (0, 0, lines), (2, early, lines - early))

    def move(n, refs=None):
        block, begin_at, size = pieces[n]
        at = pl.multiple_of(jnp.where(forward, begin_at, lines - begin_at - size), early)
        to = ext_ref.at[pl.ds(block * lines + at, size)]
        if block == 0:
            source = sib_ref
        elif block == 1:
            source = own_ref.at[pl.ds(at, size), 0:cols]
        elif refs is None:
            source = own_ref.at[pl.ds(0, size), 0:cols]
        elif len(refs) == 2:
            source = refs[n // 2]
        else:
            source = refs[0].at[pl.ds(at, size)]
        return pltpu.make_async_copy(source, to, sems.at[n])

    def launch(refs):
        move(1, refs).start()
        move(3, refs).start()

    move(0).start()
    pl.when(is_near)(lambda: launch(near_refs))
    pl.when(jnp.logical_not(is_near))(lambda: launch([far_ref]))
    move(2).start()
    outer, guard = boxes(cols, last_col)
    box_ref[...] = jnp.concatenate([outer, -outer, -guard, guard], axis=1).astype(BF16)
    acc_ref[...] = start_ref[...]
    w_ref[...] = jnp.concatenate([hi_ref[...], lo_ref[...], hi_ref[...]], axis=1)
    ext_ref[3 * lines] = jnp.zeros((cols, bands), BF16)
    if cols < out_ref.shape[1]:
        out_ref[...] = jnp.zeros(out_ref.shape, F32)
    col_id = iota((cols, 1), 0)
    outer_c = span(jnp.maximum(col_id - OUTER, 0), jnp.minimum(col_id + OUTER, last_col - 1)).astype(F32)
    guard_c = span(jnp.maximum(col_id - GUARD, 0), jnp.minimum(col_id + GUARD, last_col - 1)).astype(F32)

    def load(j):
        return ext_ref[slab_index(j, lines, last_line, index)]

    def deviation(i):
        own = lines + i
        moved = [load(own + OUTER), load(own - OUTER - 1), load(own + GUARD), load(own - GUARD - 1)]
        cycle = acc_ref[...] + jnp.dot(
            box_ref[...], jnp.concatenate(moved, axis=0), preferred_element_type=F32
        )
        acc_ref[...] = cycle
        place = jnp.where(forward, i, lines - 1 - i)
        line = index * lines + place
        outer_l = span(jnp.maximum(line - OUTER, 0), jnp.minimum(line + OUTER, last_line - 1)).astype(F32)
        guard_l = span(jnp.maximum(line - GUARD, 0), jnp.minimum(line + GUARD, last_line - 1)).astype(F32)
        counts = jnp.maximum(outer_l * outer_c - guard_l * guard_c, 1.0)
        return ext_ref[lines + place].astype(F32) - cycle * (1.0 / counts)

    def prepare(t):
        dev = jnp.concatenate([deviation(group * t + n) for n in range(group)], axis=0)
        high = dev.astype(BF16)
        dev_ref[:, :bands] = high
        dev_ref[:, bands:] = (dev - high.astype(F32)).astype(BF16)

    def finish(t):
        high = dev_ref[:, :bands]
        both = jnp.concatenate([high, high, dev_ref[:, bands:]], axis=1)
        white = lax.dot_general(w_ref[...], both, NT, preferred_element_type=F32)
        score = jnp.sum(white * white, axis=0, keepdims=True) * (1.0 / bands)
        for n in range(group):
            i = jnp.maximum(group * t + n, 0)
            place = jnp.where(forward, i, lines - 1 - i)
            good = (iota((1, cols), 1) < last_col) & (index * lines + place < last_line)
            out_ref[pl.ds(place, 1), 0:cols] = jnp.where(good, score[:, n * cols : (n + 1) * cols], 0.0)

    last = lines // group - 1

    def step(t, carry):
        @pl.when(t == early // group)
        def _():
            move(3).wait()

        finish(t - 1)
        prepare(jnp.minimum(t, last))
        return carry

    dev_ref[...] = jnp.zeros(dev_ref.shape, BF16)
    for n in range(3):
        move(n).wait()
    lax.fori_loop(0, last + 2, step, 0)


def scores(rows, columns, own, sib, near, far, start, high, low):
    lines, width, bands = own.shape
    cols = sib.shape[1]
    count = len(near)

    def kernel(rows_ref, cols_ref, own_ref, sib_ref, *rest):
        score_kernel(rest[:count], rows_ref, cols_ref, own_ref, sib_ref, *rest[count:])

    return pl.pallas_call(
        kernel,
        out_shape=jax.ShapeDtypeStruct((lines, width), F32),
        in_specs=[SMEM, SMEM] + [HBM] * (3 + count) + [VMEM] * 3,
        out_specs=VMEM,
        scratch_shapes=[
            pltpu.VMEM((3 * lines + 1, cols, bands), BF16),
            pltpu.VMEM((cols, bands), F32),
            pltpu.VMEM((cols, 4 * cols), BF16),
            pltpu.VMEM((GROUP * cols, 2 * bands), BF16),
            pltpu.VMEM((bands, 3 * bands), BF16),
            pltpu.SemaphoreType.DMA((4,)),
        ],
        compiler_params=pltpu.CompilerParams(vmem_limit_bytes=20 << 20),
        name="scores",
    )(rows, columns, own, sib, *near, far, start, high, low)


def program(cols, pixels, rows, columns):
    count = lax.axis_size("lines")
    after = lambda x, y: lax.optimization_barrier((x, y))
    swap = lambda m: [(i, i ^ m) for i in range(count)]
    both = lambda pairs: pairs + [(b, a) for a, b in pairs]

    def send(x, pairs):
        return lax.ppermute(x, "lines", pairs)

    inner = both([(i, i + 1) for i in range(1, count - 1, 4)])
    _, width, _ = pixels.shape
    near = []
    if cols > 80:
        first, rest = halves(pixels, cols)
        near.append(send(first, inner))
    if cols == width:
        used = pixels
        mine, theirs = gram_parts(rows, columns, pixels, cols)
    else:
        mine, theirs, used = gram_parts(rows, columns, pixels, cols)
    mine = mine + send(theirs, swap(1))
    if not near:
        rest = used
    used, mine = after(used, mine)
    sib = send(used, swap(1))
    near.append(send(rest, inner))
    mine = mine + send(mine, swap(2))
    step = 4
    while 2 * step < count:
        mine = mine + send(mine, swap(step))
        step *= 2
    block, mine = after(used, mine)
    mine = mine + send(mine, swap(step))
    far = send(block, both([(i, i + 1) for i in range(3, count - 1, 4)]))
    other = send(mine, swap(1))
    start = begin(rows, columns, pixels, sib, cols)
    high, low = whitening(rows, columns, mine, other)
    return scores(rows, columns, pixels, sib, near, far, start, high, low)


def solution(mesh):
    in_specs = (P(("scene", "lines"), None, None), P("scene"), P("scene"))
    out_specs = P(("scene", "lines"), None)

    def body(pixels, rows, columns):
        width = pixels.shape[1]
        sizes = [c for c in range(64, width, 16)] + [width]
        branches = [functools.partial(program, c) for c in sizes]
        choice = sum((columns[0] > c).astype(jnp.int32) for c in sizes[:-1])
        return lax.switch(choice, branches, pixels, rows, columns)

    return jax.shard_map(body, mesh=mesh, in_specs=in_specs, out_specs=out_specs, check_vma=False)
```

```python
import functools

import jax
import jax.numpy as jnp
from jax import lax
from jax.experimental import pallas as pl
from jax.experimental.pallas import tpu as pltpu
from jax.sharding import PartitionSpec as P


OUTER = 32
GUARD = 4
PANEL = 32
GROUP = 4
STEP = 16
F32 = jnp.float32
BF16 = jnp.bfloat16
HIGH = lax.Precision.HIGHEST
SMEM = pl.BlockSpec(memory_space=pltpu.SMEM)
VMEM = pl.BlockSpec(memory_space=pltpu.VMEM)
HBM = pl.BlockSpec(memory_space=pl.ANY)
TN = (((0,), (0,)), ((), ()))
NT = (((1,), (1,)), ((), ()))


def iota(shape, dim):
    return lax.broadcasted_iota(jnp.int32, shape, dim)


def gram_kernel(rows_ref, cols_ref, x_ref, keep_ref, send_ref, *rest):
    *used_ref, acc_ref, sum_ref = rest
    step = pl.program_id(0)
    lines, cols, bands = x_ref.shape
    half = bands // 2
    index = lax.axis_index("lines")
    first_line = index * lines * pl.num_programs(0)
    if used_ref:
        used_ref[0][...] = x_ref[...]
    col_mask = jnp.where(iota((cols, bands), 0) < cols_ref[0], 1.0, 0.0)
    parts = []
    for i in range(lines):
        ok = jnp.where(first_line + step * lines + i < rows_ref[0], 1.0, 0.0)
        parts.append(x_ref[i] * (col_mask * ok).astype(BF16))
    block = jnp.concatenate(parts, axis=0)
    gram = lax.dot_general(block, block, TN, preferred_element_type=F32)
    sums = jnp.dot(jnp.ones((8, lines * cols), BF16), block, preferred_element_type=F32)

    @pl.when(step == 0)
    def _():
        acc_ref[...] = gram
        sum_ref[...] = sums

    @pl.when(step > 0)
    def _():
        acc_ref[...] += gram
        sum_ref[...] += sums

    @pl.when(step == pl.num_programs(0) - 1)
    def _():
        row = iota((half, half), 0)
        col = iota((half, half), 1)
        a22 = acc_ref[half:, half:]
        diag = jnp.sum(jnp.where(row == col, a22, 0.0), axis=0, keepdims=True)
        mixed = jnp.where(row <= col, acc_ref[:half, :half], a22)
        slot = iota((8, half), 0)
        tail = jnp.where(slot == 0, sum_ref[0:1, :half], jnp.where(slot == 1, sum_ref[0:1, half:], 0.0))
        diag = jnp.where(slot == 0, diag, 0.0)
        first = index % 2 == 0
        cross = acc_ref[:half, half:]
        keep_ref[:half] = jnp.where(first, cross, mixed)
        send_ref[:half] = jnp.where(first, mixed, cross)
        keep_ref[half:] = jnp.where(first, tail, diag)
        send_ref[half:] = jnp.where(first, diag, tail)


def gram_parts(rows, columns, pixels, cols):
    lines, width, bands = pixels.shape
    half = bands // 2
    step = min(lines, STEP)
    block = pl.BlockSpec((step, cols, bands), lambda i: (i, 0, 0))
    part = pl.BlockSpec((half + 8, half), lambda i: (0, 0))
    shapes = [jax.ShapeDtypeStruct((half + 8, half), F32)] * 2
    specs = [part, part]
    if cols < width:
        shapes.append(jax.ShapeDtypeStruct((lines, cols, bands), pixels.dtype))
        specs.append(block)
    return pl.pallas_call(
        gram_kernel,
        out_shape=shapes,
        grid=(lines // step,),
        in_specs=[SMEM, SMEM, block],
        out_specs=specs,
        scratch_shapes=[pltpu.VMEM((bands, bands), F32), pltpu.VMEM((8, bands), F32)],
        compiler_params=pltpu.CompilerParams(vmem_limit_bytes=16 << 20),
        name="gram",
    )(rows, columns, pixels)


def halves_kernel(x_ref, first_ref, rest_ref, sems):
    size, cols, _ = first_ref.shape
    odd = lax.axis_index("lines") % 2
    copies = []
    for n, ref in enumerate((first_ref, rest_ref)):
        at = pl.multiple_of(jnp.where(odd == n, 0, 1) * size, size)
        copies.append(pltpu.make_async_copy(x_ref.at[pl.ds(at, size), 0:cols], ref, sems.at[n]))
    for copy in copies:
        copy.start()
    for copy in copies:
        copy.wait()


def halves(pixels, cols):
    lines, _, bands = pixels.shape
    shape = jax.ShapeDtypeStruct((lines // 2, cols, bands), pixels.dtype)
    return pl.pallas_call(
        halves_kernel,
        out_shape=(shape, shape),
        in_specs=[HBM],
        out_specs=(VMEM, VMEM),
        scratch_shapes=[pltpu.SemaphoreType.DMA((2,))],
        compiler_params=pltpu.CompilerParams(vmem_limit_bytes=8 << 20),
        name="halves",
    )(pixels)


def eliminate(x_ref, rolled):
    half = x_ref.shape[0] // 2
    sub = iota((PANEL, half), 0)
    lane = iota((PANEL, half), 1)

    def panel_pass(side, left):
        base = pl.multiple_of(side * half, half)
        away = pl.multiple_of((1 - side) * half, half)
        both = (pl.ds(base, half), pl.ds(away, half))
        rows_at = pl.ds(pl.multiple_of(base + left, PANEL), PANEL)
        tiles = [x_ref[rows_at, at] for at in both]
        turned, offset = tiles[0], left
        if rolled:
            turned, offset = pltpu.roll(tiles[0], (half - left) % half, 1), 0
        norm = jnp.ones((PANEL, half), F32)
        columns = []
        for j in range(PANEL):
            top = j - j % 8
            columns.append(jnp.broadcast_to(turned[top:, offset + j : offset + j + 1], (PANEL - top, half)))
        for j in range(PANEL):
            top = j - j % 8
            column = columns[j]
            pivot = column[j - top : j - top + 1, :]
            rows = sub[top:]
            factor = jnp.where(rows > j, column * (1.0 / pivot), 0.0)
            for n in range(j + 1, PANEL):
                skip = n - n % 8
                columns[n] = columns[n] - factor[skip - top :] * column[n - top : n - top + 1, :]
            norm = jnp.where(sub == j, lax.rsqrt(pivot), norm)
            for q in range(2):
                row = tiles[q][j : j + 1, :]
                old = tiles[q][top:]
                if q == 0:
                    row = jnp.where(lane[0:1] == left + j, 1.0, row)
                    here = (lane[top:] == left + j) & (rows >= j)
                    old = jnp.where(here, jnp.where(rows == j, 1.0, 0.0), old)
                new = old - factor * row
                tiles[q] = new if top == 0 else jnp.concatenate([tiles[q][:top], new], axis=0)
        tiles = [tile * norm for tile in tiles]
        tiles[0] = jnp.where((lane > left + sub) & (lane < left + PANEL), 0.0, tiles[0])
        for tile, at in zip(tiles, both):
            x_ref[rows_at, at] = tile
        panel = jnp.concatenate(tiles, axis=1)
        end = left + PANEL
        lane_r = iota((half, half), 1)
        block = (lane_r >= left) & (lane_r < end)
        if rolled:
            update = lax.dot_general(tiles[0], panel, TN, precision=HIGH, preferred_element_type=F32)
            later = iota((half, half), 0) >= end
            for q in range(2):
                old = x_ref[both[0], both[q]]
                new = (jnp.where(block, 0.0, old) if q == 0 else old) - update[:, q * half : (q + 1) * half]
                x_ref[both[0], both[q]] = jnp.where(later, new, old)
        elif end < half:
            update = lax.dot_general(tiles[0], panel, TN, precision=HIGH, preferred_element_type=F32)
            rest_at = pl.ds(pl.multiple_of(base + end, PANEL), half - end)
            rest = jnp.where(block[end:], 0.0, x_ref[rest_at, both[0]])
            x_ref[rest_at, both[0]] = rest - update[end:, :half]
            x_ref[rest_at, both[1]] = x_ref[rest_at, both[1]] - update[end:, half:]
        update = lax.dot_general(tiles[1], panel, TN, precision=HIGH, preferred_element_type=F32)
        below = side == 0
        for q in range(2):
            old = x_ref[both[1], both[q]]
            new = (jnp.where(block, 0.0, old) if q == 0 else old) - update[:, q * half : (q + 1) * half]
            x_ref[both[1], both[q]] = jnp.where(below, new, old)

    def side_pass(side, carry):
        for left in range(0, half, PANEL):
            panel_pass(side, left)
        return carry

    def one_pass(k, carry):
        per = half // PANEL
        panel_pass(k // per, k % per * PANEL)
        return carry

    if rolled:
        lax.fori_loop(0, 2 * half // PANEL, one_pass, 0)
    else:
        lax.fori_loop(0, 2, side_pass, 0)


def whiten_kernel(rolled, rows_ref, cols_ref, mine_ref, other_ref, out_ref, x_ref):
    half = mine_ref.shape[1]
    bands = 2 * half
    first = lax.axis_index("lines") % 2 == 0
    total = jnp.full((1, 1), rows_ref[0] * cols_ref[0], jnp.int32).astype(F32)
    cross = jnp.where(first, mine_ref[:half], other_ref[:half])
    mixed = jnp.where(first, other_ref[:half], mine_ref[:half])
    tail = jnp.where(first, mine_ref[half:], other_ref[half:])
    diag = jnp.where(first, other_ref[half:], mine_ref[half:])
    row = iota((half, half), 0)
    col = iota((half, half), 1)
    mixed_t = mixed.T
    a11 = jnp.where(row <= col, mixed, mixed_t)
    a22 = jnp.where(row > col, mixed, jnp.where(row == col, diag[0:1], mixed_t))
    sums = jnp.concatenate([tail[0:1], tail[1:2]], axis=1)
    sums = jnp.where(iota((8, bands), 0) == 0, sums, 0.0)
    outer = lax.dot_general(sums, sums / total, TN, precision=HIGH, preferred_element_type=F32)
    scale = 1.0 / (total - 1.0)
    x_ref[:half, :half] = (a11 - outer[:half, :half]) * scale
    x_ref[:half, half:] = (cross - outer[:half, half:]) * scale
    x_ref[half:, half:] = (a22 - outer[half:, half:]) * scale
    x_ref[half:, :half] = jnp.zeros((half, half), F32)
    eliminate(x_ref, rolled)
    full = x_ref[...]
    whiten = jnp.where(iota((bands, bands), 1) <= iota((bands, bands), 0), full, 0.0)
    high = whiten.astype(BF16)
    out_ref[:, :bands] = high
    out_ref[:, bands : 2 * bands] = (whiten - high.astype(F32)).astype(BF16)
    out_ref[:, 2 * bands :] = high


def whitening(rows, columns, mine, other, rolled):
    half = mine.shape[1]
    bands = 2 * half
    return pl.pallas_call(
        functools.partial(whiten_kernel, rolled),
        out_shape=jax.ShapeDtypeStruct((bands, 3 * bands), BF16),
        in_specs=[SMEM, SMEM, VMEM, VMEM],
        out_specs=VMEM,
        scratch_shapes=[pltpu.VMEM((bands, bands), F32)],
        compiler_params=pltpu.CompilerParams(vmem_limit_bytes=8 << 20),
        name="whiten",
    )(rows, columns, mine, other)


def boxes(cols, last_col):
    row = iota((cols, cols), 0)
    col = iota((cols, cols), 1)
    inside = col < last_col
    outer = jnp.where(inside & (jnp.abs(row - col) <= OUTER), 1.0, 0.0)
    guard = jnp.where(inside & (jnp.abs(row - col) <= GUARD), 1.0, 0.0)
    return outer, guard


def slab_index(j, lines, last_line, index):
    forward = index % 2 == 1
    within = jnp.bitwise_and(j, lines - 1)
    part = (j + lines) // lines - 1
    place = jnp.where(forward, within, lines - 1 - within)
    start = (index + jnp.where(forward, part - 1, 1 - part)) * lines
    return jnp.where((j >= 0) & (start + place < last_line), part * lines + place, 3 * lines)


def begin_kernel(rows_ref, cols_ref, own_ref, sib_ref, out_ref, ext_ref, sums_ref, sems):
    lines = own_ref.shape[0]
    cols, bands = out_ref.shape
    last_line, last_col = rows_ref[0], cols_ref[0]
    index = lax.axis_index("lines")
    copies = [
        pltpu.make_async_copy(sib_ref, ext_ref.at[0:lines], sems.at[0]),
        pltpu.make_async_copy(own_ref.at[:, 0:cols], ext_ref.at[lines : 2 * lines], sems.at[1]),
    ]
    for copy in copies:
        copy.start()
    outer, guard = boxes(cols, last_col)
    box = jnp.concatenate([outer, -guard, outer, -guard], axis=1).astype(BF16)
    for copy in copies:
        copy.wait()
    other = index + jnp.where(index % 2 == 0, 1, -1)
    for part, owner in enumerate((other, index)):

        def clear(i, carry, part=part):
            ext_ref[part * lines + i] = jnp.zeros((cols, bands), BF16)
            return carry

        lax.fori_loop(jnp.clip(last_line - owner * lines, 0, lines), lines, clear, 0)
    strip = 32 if cols % 32 == 0 else 16
    near_by = [slab_index(j, lines, 1 << 30, index) for j in range(lines - GUARD - 1, lines + GUARD)]
    for r in range(0, cols, strip):

        def add(j, acc, r=r):
            return acc + ext_ref[j, r : r + strip, :].astype(F32)

        total = lax.fori_loop(0, 2 * lines, add, jnp.zeros((strip, bands), F32), unroll=16)
        close = ext_ref[near_by[0], r : r + strip, :].astype(F32)
        for place in near_by[1:]:
            close = close + ext_ref[place, r : r + strip, :].astype(F32)
        for base, value in ((0, total), (cols, close)):
            high = value.astype(BF16)
            sums_ref[base + r : base + r + strip, :] = high
            sums_ref[base + r + 2 * cols : base + r + 2 * cols + strip, :] = (value - high.astype(F32)).astype(BF16)
    out_ref[...] = jnp.dot(box, sums_ref[...], preferred_element_type=F32)


def begin(rows, columns, own, sib, cols):
    lines, _, bands = own.shape
    return pl.pallas_call(
        begin_kernel,
        out_shape=jax.ShapeDtypeStruct((cols, bands), F32),
        in_specs=[SMEM, SMEM, HBM, HBM],
        out_specs=VMEM,
        scratch_shapes=[
            pltpu.VMEM((2 * lines, cols, bands), BF16),
            pltpu.VMEM((4 * cols, bands), BF16),
            pltpu.SemaphoreType.DMA((2,)),
        ],
        compiler_params=pltpu.CompilerParams(vmem_limit_bytes=12 << 20),
        name="begin",
    )(rows, columns, own, sib)


def span(low, high):
    return jnp.maximum(high - low + 1, 0)


def score_kernel(half, near_refs, far_refs, rows_ref, cols_ref, own_ref, sib_ref, start_ref, w_ref, *rest):
    prior_ref = rest[:-6]
    out_ref, acc_ref, ext_ref, box_ref, dev_ref, sems = rest[-6:]
    lines = own_ref.shape[0]
    _, cols, bands = ext_ref.shape
    last_line, last_col = rows_ref[0], cols_ref[0]
    index = lax.axis_index("lines")
    forward = index % 2 == 1
    is_near = (index % 4 == 1) | (index % 4 == 2)
    group = dev_ref.shape[0] // cols

    early = lines // 2
    pieces = [(1, 0, lines), (2, 0, early), (0, 0, lines), (2, early, lines - early)]
    if half == 0:
        pieces.pop()

    def move(n, refs=None):
        block, begin_at, size = pieces[n]
        at = pl.multiple_of(jnp.where(forward, begin_at, lines - begin_at - size), early)
        to = ext_ref.at[pl.ds(block * lines + at, size)]
        if block == 0:
            source = sib_ref
        elif block == 1:
            source = own_ref.at[pl.ds(at, size), 0:cols]
        elif refs is None:
            source = own_ref.at[pl.ds(0, size), 0:cols]
        elif refs[0].shape[0] == lines:
            source = refs[0].at[pl.ds(at, size)]
        else:
            source = refs[n // 2]
        return pltpu.make_async_copy(source, to, sems.at[n])

    def launch(refs):
        for n in range(1, len(pieces), 2):
            move(n, refs).start()

    move(0).start()
    pl.when(is_near)(lambda: launch(near_refs))
    pl.when(jnp.logical_not(is_near))(lambda: launch(far_refs))
    move(2).start()
    outer, guard = boxes(cols, last_col)
    box_ref[...] = jnp.concatenate([outer, -outer, -guard, guard], axis=1).astype(BF16)
    acc_ref[...] = start_ref[...]
    ext_ref[3 * lines] = jnp.zeros((cols, bands), BF16)
    out_ref[...] = prior_ref[0][...] if half else jnp.zeros(out_ref.shape, F32)
    col_id = iota((cols, 1), 0)
    outer_c = span(jnp.maximum(col_id - OUTER, 0), jnp.minimum(col_id + OUTER, last_col - 1)).astype(F32)
    guard_c = span(jnp.maximum(col_id - GUARD, 0), jnp.minimum(col_id + GUARD, last_col - 1)).astype(F32)

    def load(j):
        return ext_ref[slab_index(j, lines, last_line, index)]

    def deviation(i):
        own = lines + i
        moved = [load(own + OUTER), load(own - OUTER - 1), load(own + GUARD), load(own - GUARD - 1)]
        cycle = acc_ref[...] + jnp.dot(
            box_ref[...], jnp.concatenate(moved, axis=0), preferred_element_type=F32
        )
        acc_ref[...] = cycle
        place = jnp.where(forward, i, lines - 1 - i)
        line = index * lines + place
        outer_l = span(jnp.maximum(line - OUTER, 0), jnp.minimum(line + OUTER, last_line - 1)).astype(F32)
        guard_l = span(jnp.maximum(line - GUARD, 0), jnp.minimum(line + GUARD, last_line - 1)).astype(F32)
        counts = jnp.maximum(outer_l * outer_c - guard_l * guard_c, 1.0)
        return ext_ref[lines + place].astype(F32) - cycle * (1.0 / counts)

    def prepare(t):
        dev = jnp.concatenate([deviation(group * t + n) for n in range(group)], axis=0)
        high = dev.astype(BF16)
        dev_ref[:, :bands] = high
        dev_ref[:, bands:] = (dev - high.astype(F32)).astype(BF16)

    first = early // group if half else 0
    end = early // group if half == 0 else lines // group

    def finish(t):
        high = dev_ref[:, :bands]
        both = jnp.concatenate([high, high, dev_ref[:, bands:]], axis=1)
        white = lax.dot_general(w_ref[...], both, NT, preferred_element_type=F32)
        score = jnp.sum(white * white, axis=0, keepdims=True) * (1.0 / bands)
        for n in range(group):
            i = jnp.maximum(group * t + n, group * first)
            place = jnp.where(forward, i, lines - 1 - i)
            good = (iota((1, cols), 1) < last_col) & (index * lines + place < last_line)
            out_ref[pl.ds(place, 1), 0:cols] = jnp.where(good, score[:, n * cols : (n + 1) * cols], 0.0)

    middle = early // group

    def step(t, carry):
        if half is None:

            @pl.when(t == middle)
            def _():
                move(3).wait()

        finish(t - 1)
        prepare(t)
        return carry

    dev_ref[...] = jnp.zeros(dev_ref.shape, BF16)
    for n in range(3 if half is None else len(pieces)):
        move(n).wait()
    lax.fori_loop(first, end, step, 0)
    finish(end - 1)


def scores(half, rows, columns, own, sib, near, far, start, factor, *prior):
    lines, width, bands = own.shape
    cols = sib.shape[1]
    count = len(near)
    both = count + len(far)
    group = 2 * GROUP if half is None else GROUP

    def kernel(rows_ref, cols_ref, own_ref, sib_ref, *rest):
        score_kernel(half, rest[:count], rest[count:both], rows_ref, cols_ref, own_ref, sib_ref, *rest[both:])

    return pl.pallas_call(
        kernel,
        out_shape=(jax.ShapeDtypeStruct((lines, width), F32), jax.ShapeDtypeStruct((cols, bands), F32)),
        in_specs=[SMEM, SMEM] + [HBM] * (2 + count + len(far)) + [VMEM] * (2 + len(prior)),
        out_specs=(VMEM, VMEM),
        scratch_shapes=[
            pltpu.VMEM((3 * lines + 1, cols, bands), BF16),
            pltpu.VMEM((cols, 4 * cols), BF16),
            pltpu.VMEM((group * cols, 2 * bands), BF16),
            pltpu.SemaphoreType.DMA((4,)),
        ],
        compiler_params=pltpu.CompilerParams(vmem_limit_bytes=20 << 20),
        name="scores",
    )(rows, columns, own, sib, *near, *far, start, factor, *prior)


def program(cols, pixels, rows, columns):
    count = lax.axis_size("lines")
    after = lambda x, y: lax.optimization_barrier((x, y))
    swap = lambda m: [(i, i ^ m) for i in range(count)]
    both = lambda pairs: pairs + [(b, a) for a, b in pairs]

    def send(x, pairs):
        return lax.ppermute(x, "lines", pairs)

    inner = both([(i, i + 1) for i in range(1, count - 1, 4)])
    _, width, _ = pixels.shape
    near = []
    if cols > 80:
        first, rest = halves(pixels, cols)
        near.append(send(first, inner))
    if cols == width:
        used = pixels
        mine, theirs = gram_parts(rows, columns, pixels, cols)
    else:
        mine, theirs, used = gram_parts(rows, columns, pixels, cols)
    mine = mine + send(theirs, swap(1))
    if not near:
        rest = used
    used, mine = after(used, mine)
    sib = send(used, swap(1))
    near.append(send(rest, inner))
    mine = mine + send(mine, swap(2))
    step = 4
    while 2 * step < count:
        mine = mine + send(mine, swap(step))
        step *= 2
    wide = len(near) > 1
    parts = [first, rest] if wide else [used]
    for n, part in enumerate(parts):
        parts[n], mine = after(part, mine)
    mine = mine + send(mine, swap(step))
    cross = both([(i, i + 1) for i in range(3, count - 1, 4)])
    far = [send(part, cross) for part in parts]
    other = send(mine, swap(1))
    acc = begin(rows, columns, pixels, sib, cols)
    factor = whitening(rows, columns, mine, other, wide)
    shared = (rows, columns, pixels, sib)
    if not wide:
        return scores(None, *shared, near, far, acc, factor)[0]
    out, acc = scores(0, *shared, near[:1], far[:1], acc, factor)
    return scores(1, *shared, near, far, acc, factor, out)[0]


def solution(mesh):
    in_specs = (P(("scene", "lines"), None, None), P("scene"), P("scene"))
    out_specs = P(("scene", "lines"), None)

    def body(pixels, rows, columns):
        width = pixels.shape[1]
        sizes = [c for c in range(64, width, 16)] + [width]
        branches = [functools.partial(program, c) for c in sizes]
        choice = sum((columns[0] > c).astype(jnp.int32) for c in sizes[:-1])
        return lax.switch(choice, branches, pixels, rows, columns)

    return jax.shard_map(body, mesh=mesh, in_specs=in_specs, out_specs=out_specs, check_vma=False)
```
